32 devices in a mesh: ctx: 16 (over z, x, core), tp: 2 (over y).
Axes of the slice: x: 2, y: 2, z: 4, core: 2. Of those that a mesh axis runs over, the one named last changes fastest.
Arguments:
- token_ids: int32 [8192], P('ctx'), may hold values from 0 to 511
- embed_table: bfloat16 [512, 8192], P(None, 'tp'), may hold values from -81 to 81
- projected_table: bfloat16 [512, 3, 8192], P(None, None, 'tp'), may hold values from -10.5 to 10.5
- feat_one: float32 [3, 3, 8192], P(None, None, 'tp'), may hold values from -3 to 3
- inner_taps: float32 [7, 8192], P(None, 'tp'), may hold values from -2 to 2
- feat_two: float32 [3, 3, 8192], P(None, None, 'tp'), may hold values from -3 to 3
- decay: float32 [8192, 16], P('tp'), may hold values from 3.540039e-05 to 0.03448276
- residue: float32 [8192, 16], P('tp'), may hold values from -0.26261287 to 0.26261287
Outputs:
- stream_out: bfloat16 [8192, 8192], P('ctx', 'tp')
The draws below stay inside these ranges and needn't reach their ends.
All inputs are finite; a program needn't handle non-finite values.
Results may differ from the reference program's by a relative error of at most 0.0048.
Values may be sent and summed in bfloat16 or wider, within the bound.
A program may use at most 320 MiB of HBM per device.

```python
import math
import jax
import jax.numpy as jnp
import numpy as np
from jax import lax

D = 8192
VOCAB = 512
FEAT_TAPS = 3
SHORT_TAPS = 7
MODES = 16
TOKENS = 8192


def draw_embed_table(key, part):
    subkeys = jax.random.split(jax.random.fold_in(key, 11), 3)
    column = jnp.arange(D, dtype=jnp.int32).astype(jnp.float32)
    rising = 4.0 ** (column / D - 0.5)
    row_scale = jnp.exp(jax.random.uniform(subkeys[1], (VOCAB, 1), jnp.float32) * math.log(10.0))
    col_scale = jnp.exp(jax.random.uniform(subkeys[2], (1, D), jnp.float32) * math.log(10.0))
    entries = jnp.clip(jax.random.normal(subkeys[0], (VOCAB, D), jnp.float32), -4.0, 4.0)
    return (entries * row_scale * col_scale * rising[None, :] / 10.0).astype(jnp.bfloat16)


def draw_projected_table(key, part):
    subkeys = jax.random.split(jax.random.fold_in(key, 23), 3)
    row_scale = jnp.exp(jax.random.uniform(subkeys[1], (VOCAB, 1, 1), jnp.float32, math.log(0.6), math.log(1.6)))
    col_scale = jnp.exp(jax.random.uniform(subkeys[2], (1, 3, D), jnp.float32, math.log(0.6), math.log(1.6)))
    entries = jnp.clip(jax.random.normal(subkeys[0], (VOCAB, 3, D), jnp.float32), -4.0, 4.0)
    return (entries * row_scale * col_scale).astype(jnp.bfloat16)


def mode_draw(key):
    subkeys = jax.random.split(jax.random.fold_in(key, 37), 4)
    slow_share = 0.5
    chooser = jax.random.uniform(subkeys[0], (D, 1), jnp.float32)
    slow_rates = jnp.exp(jax.random.uniform(subkeys[1], (D, MODES), jnp.float32, math.log(0.3 / TOKENS), math.log(2.0 / TOKENS)))
    fast_rates = jnp.exp(jax.random.uniform(subkeys[2], (D, MODES), jnp.float32, math.log(1.0 / 50.0), math.log(1.0 / 30.0)))
    decays = jnp.where(chooser < slow_share, slow_rates, fast_rates)
    weights = jnp.clip(jax.random.normal(subkeys[3], (D, MODES), jnp.float32), -4.0, 4.0) * jnp.sqrt(2.0 * decays / MODES)
    return (decays, weights)


def draw_decay(key, part):
    return mode_draw(key)[0]


def draw_residue(key, part):
    return mode_draw(key)[1]


def set_ends(values, own_key, low, largest):
    longest = values.shape.index(max(values.shape))
    spots = []
    for shift in (0, 1):
        where = [jax.random.randint(jax.random.fold_in(own_key, axis), (), 0, length) for axis, length in enumerate(values.shape)]
        where[longest] = (where[longest] + shift) % values.shape[longest]
        spots.append(tuple(where))
    return values.at[spots[0]].set(low).at[spots[1]].set(largest)


def steps_of(key, extent, cuts, smallest, largest):
    def one(axis_at, parts):
        draws = jax.random.uniform(jax.random.fold_in(jax.random.fold_in(key, 6), axis_at), (parts,), jnp.float32, smallest / len(cuts), largest / len(cuts))
        return jnp.repeat(jnp.exp(draws), extent[axis_at] // parts).reshape((-1,) + (1,) * (len(extent) - axis_at - 1))

    loudness = one(*cuts[0])
    for cut in cuts[1:]:
        loudness = loudness * one(*cut)
    return loudness


def cumulative_ranks(amount, slope):
    portions = [(1 << 20) // math.isqrt(grade ** slope) + 1 for grade in range(1, amount + 1)]
    width = 1 + sum(portions) // (1 << 30)
    return np.cumsum(np.array([max(1, weight // width) for weight in portions]))


def skewed_ids(stream_key, extent, number_of, skew):
    listing = cumulative_ranks(number_of, skew)
    ticket = jax.random.randint(jax.random.fold_in(stream_key, 1), extent, 0, int(listing[number_of - 1]))
    rank = jnp.searchsorted(jnp.asarray(listing, jnp.int32), ticket, side="right")
    return jax.random.permutation(jax.random.fold_in(stream_key, 2), number_of)[rank].astype(jnp.int32)


def centred(own_key, dims, deviation, limit, cuts=(), kind=jnp.bfloat16):
    values = jax.random.normal(own_key, dims, jnp.float32) * deviation
    if len(cuts) > 0:
        values = steps_of(own_key, dims, cuts, -0.22, 0.18) * values
    return jnp.clip(values, min=-limit, max=limit).astype(kind)


def setup_inputs(seed: int = 0) -> dict:
    arg_keys = jax.random.split(jax.random.key(seed), 9)
    return {
        "token_ids": set_ends(skewed_ids(arg_keys[0], (TOKENS,), VOCAB, 2), jax.random.fold_in(arg_keys[0], 3), 0, VOCAB - 1).astype(jnp.int32),
        "embed_table": draw_embed_table(jax.random.fold_in(arg_keys[8], 71), 0),
        "projected_table": draw_projected_table(jax.random.fold_in(arg_keys[8], 71), 0),
        "feat_one": centred(arg_keys[3], (FEAT_TAPS, 3, D), 0.6, 3.0, ((2, 2),), jnp.float32),
        "inner_taps": centred(arg_keys[4], (SHORT_TAPS, D), 0.4, 2.0, ((1, 2),), jnp.float32),
        "feat_two": centred(arg_keys[5], (FEAT_TAPS, 3, D), 0.6, 3.0, ((2, 2),), jnp.float32),
        "decay": draw_decay(jax.random.fold_in(arg_keys[8], 71), 0),
        "residue": draw_residue(jax.random.fold_in(arg_keys[8], 71), 0),
    }


epsilon = 1e-06

def causal_taps(series, weights):
    tap_count = weights.shape[0]
    length = series.shape[0]
    padded = jnp.concatenate([jnp.zeros((tap_count - 1,) + series.shape[1:], series.dtype), series], axis=0)
    summed = jnp.zeros_like(series)
    for offset in range(tap_count):
        summed = summed + weights[offset] * padded[tap_count - 1 - offset:tap_count - 1 - offset + length]
    return summed

def by_blocks(array, axis, blocks):
    reordered = jnp.moveaxis(array, axis, -1)
    reordered = reordered.reshape(reordered.shape[:-1] + (blocks, reordered.shape[-1] // blocks))
    return jnp.moveaxis(reordered, -2, 0)

def reference(token_ids, embed_table, projected_table, feat_one, inner_taps, feat_two, decay, residue):
    blocks = 16
    length = token_ids.shape[0]
    positions = jnp.arange(length).astype(jnp.float32)

    def first_block(pieces):
        emb_piece, proj_piece, feat_piece, inner_piece = pieces
        embedded = jnp.take(emb_piece, token_ids, axis=0).astype(jnp.float32)
        raw_rows = jnp.take(proj_piece, token_ids, axis=0).astype(jnp.float32)
        queries = causal_taps(raw_rows[:, 0], feat_piece[:, 0])
        key_rows = causal_taps(raw_rows[:, 1], feat_piece[:, 1])
        valued = causal_taps(raw_rows[:, 2], feat_piece[:, 2])
        return (embedded + queries * causal_taps(key_rows * valued, inner_piece)).astype(jnp.bfloat16)
    stream = lax.map(first_block, (by_blocks(embed_table, 1, blocks), by_blocks(projected_table, 2, blocks), by_blocks(feat_one, 2, blocks), by_blocks(inner_taps, 1, blocks)))
    stream = jnp.moveaxis(stream, 0, 1).reshape(length, D)
    widened = stream.astype(jnp.float32)
    inverse_rms = lax.rsqrt(lax.optimization_barrier(jnp.sum(widened * widened, axis=1)) / D + epsilon)

    def second_block(pieces):
        stream_piece, feat_piece, decay_piece, residue_piece = pieces
        normed = stream_piece.astype(jnp.float32) * inverse_rms[:, None]
        queries = causal_taps(normed, feat_piece[:, 0])
        key_rows = causal_taps(normed, feat_piece[:, 1])
        valued = causal_taps(normed, feat_piece[:, 2])
        product = lax.optimization_barrier((key_rows * valued).astype(jnp.bfloat16)).astype(jnp.float32)
        response = jnp.zeros_like(normed)
        for mode_number in range(decay_piece.shape[0]):
            response = response + residue_piece[mode_number] * jnp.exp(-decay_piece[mode_number] * positions[:, None])
        padded_len = 2 * length
        spectrum = jnp.fft.rfft(product, n=padded_len, axis=0) * jnp.fft.rfft(response, n=padded_len, axis=0)
        convolved = jnp.fft.irfft(spectrum, n=padded_len, axis=0)[:length]
        return (stream_piece.astype(jnp.float32) + queries * convolved).astype(jnp.bfloat16)
    result = lax.map(second_block, (by_blocks(stream, 1, blocks), by_blocks(feat_two, 2, blocks), by_blocks(decay, 0, blocks), by_blocks(residue, 0, blocks)))
    return jnp.moveaxis(result, 0, 1).reshape(length, D)
```

```python
import functools

import jax
import jax.numpy as jnp
from jax import lax
from jax.experimental import pallas as pl
from jax.experimental.pallas import tpu as pltpu
from jax.sharding import PartitionSpec as P

epsilon = 1e-06
HALO = 16
SEGMENTS = 8
LANES = 128
VMEM_LIMIT = 60 * 1024 * 1024
MESH = pl.DeviceIdType.MESH


def even(value):
    return value + value % 2


def wide_row(ref, index):
    return jnp.broadcast_to(ref[index], (SEGMENTS, LANES))


def weighted(taps, series):
    terms = [tap * value for tap, value in zip(taps, series)]
    total = terms[0]
    for term in terms[1:]:
        total = total + term
    return total


def tree_sum(terms):
    while len(terms) > 1:
        pairs = [a + b for a, b in zip(terms[::2], terms[1::2])]
        terms = pairs + terms[2 * len(pairs) :]
    return terms[0]


def first_kernel(lead, keep, one_hot, embed, proj, feat, inner, stream, sums, raw_a, raw_b, squares):
    width = embed.shape[1]
    blocks = width // LANES
    steps = one_hot.shape[0] // SEGMENTS - lead
    reach = feat.shape[0]
    span = inner.shape[0]

    @pl.when(pl.program_id(0) == 0)
    def _():
        squares[...] = jnp.zeros_like(squares)

    def project(block, raw):
        lanes = pl.ds(pl.multiple_of(block * LANES, LANES), LANES)
        ids = one_hot[...]
        for first, tables in enumerate(
            ((embed[:, lanes], proj[0, :, lanes]), (proj[1, :, lanes], proj[2, :, lanes]))
        ):
            both = jnp.dot(
                ids, jnp.concatenate(tables, axis=1), preferred_element_type=jnp.float32
            )
            raw[2 * first] = both[:, :LANES]
            raw[2 * first + 1] = both[:, LANES:]

    def mix(block, raw):
        lanes = pl.ds(pl.multiple_of(block * LANES, LANES), LANES)
        feat_taps = [
            [wide_row(feat, (j, slice(s, s + 1), lanes)) for j in range(reach)] for s in range(3)
        ]
        inner_taps = [wide_row(inner, (slice(j, j + 1), lanes)) for j in range(span)]

        def row(s, step):
            return raw[s, pl.ds((step + lead) * SEGMENTS, SEGMENTS), :]

        mixed = []
        held = []
        pasts = [[], [], []]
        for step in range(-lead, steps):
            for s in range(3):
                if s == 0 and step < 1 - keep - reach:
                    continue
                pasts[s] = ([row(s + 1, step)] + pasts[s])[:reach]
            if step < reach - 1 - lead:
                continue
            keyed = weighted(feat_taps[1], pasts[1])
            valued = weighted(feat_taps[2], pasts[2])
            mixed = ([keyed * valued] + mixed)[:span]
            if step < -keep:
                continue
            queries = weighted(feat_taps[0], pasts[0])
            total = row(0, step) + queries * weighted(inner_taps, mixed)
            at = step + keep
            squares[pl.ds(at * SEGMENTS, SEGMENTS), :] += total * total
            held.append(total)
            if len(held) == 2:
                pair = jnp.concatenate(held, axis=0).astype(jnp.bfloat16)
                stream[pl.ds((at - 1) * SEGMENTS, 2 * SEGMENTS), lanes] = pair
                held = []

    project(0, raw_a)

    @pl.loop(0, blocks // 2)
    def _(pair):
        project(2 * pair + 1, raw_b)
        mix(2 * pair, raw_a)
        project(jnp.minimum(2 * pair + 2, blocks - 1), raw_a)
        mix(2 * pair + 1, raw_b)

    @pl.when(pl.program_id(0) == pl.num_programs(0) - 1)
    def _():
        sums[...] = lax.dot_general(
            jnp.ones((SEGMENTS, LANES), jnp.float32),
            squares[...],
            (((1,), (1,)), ((), ())),
            precision=lax.Precision.HIGHEST,
            preferred_element_type=jnp.float32,
        )


def greet(axis, count, me):
    barrier = pltpu.get_barrier_semaphore()
    for k in range(1, count):
        pl.semaphore_signal(
            barrier, inc=1, device_id={axis: lax.rem(me + k, count)}, device_id_type=MESH
        )
    pl.semaphore_wait(barrier, count - 1)


def norm_kernel(count, channels, sums, inverse, parts, send, recv):
    me = lax.axis_index("tp")
    rows = inverse.shape[0]
    greet("tp", count, me)

    def copy(slot, k, peer):
        return pltpu.make_async_remote_copy(
            src_ref=sums,
            dst_ref=parts.at[slot],
            send_sem=send.at[k],
            recv_sem=recv.at[slot],
            device_id={"tp": peer},
            device_id_type=MESH,
        )

    copies = [copy(me, k, lax.rem(me + k, count)) for k in range(1, count)]
    for one in copies:
        one.start()
    parts[me] = sums[...]
    for k in range(1, count):
        peer = lax.rem(me + k, count)
        copy(peer, k, peer).wait_recv()
    total = parts[0]
    for k in range(1, count):
        total = total + parts[k]
    row = lax.rsqrt(total / channels + epsilon)
    for at in range(0, rows, LANES):
        block = jnp.broadcast_to(row[0:1, at : at + LANES], (LANES, LANES))
        inverse[pl.ds(at, LANES), :] = jnp.transpose(block)
    for one in copies:
        one.wait_send()


def second_kernel(keep, stream, inverse, feat, slope, weight, local, states, ends, product, powers):
    width = stream.shape[1]
    steps = stream.shape[0] // SEGMENTS - keep
    modes = slope.shape[0]
    reach = feat.shape[0]
    place = lax.broadcasted_iota(jnp.int32, (SEGMENTS, LANES), 0)
    for block in range(width // LANES):
        lanes = slice(block * LANES, (block + 1) * LANES)
        taps = [
            [wide_row(feat, (j, slice(s, s + 1), lanes)) for j in range(reach)] for s in (1, 2)
        ]

        def normed_pair(at):
            where = pl.ds(pl.multiple_of(at * SEGMENTS, 2 * SEGMENTS), 2 * SEGMENTS)
            both = stream[where, lanes].astype(jnp.float32) * inverse[where, :]
            return both[:SEGMENTS], both[SEGMENTS:]

        past = ()
        for at in range(keep - even(reach - 1), keep, 2):
            past = tuple(reversed(normed_pair(at))) + past
        past = past[: reach - 1]

        def multiply(pair, past):
            first, second = normed_pair(keep + 2 * pair)
            products = []
            for value in (first, second):
                series = (value,) + past
                products.append(weighted(taps[0], series) * weighted(taps[1], series))
                past = series[: reach - 1]
            where = pl.ds(pl.multiple_of(pair * 2 * SEGMENTS, 2 * SEGMENTS), 2 * SEGMENTS)
            rounded = jnp.concatenate(products, axis=0).astype(jnp.bfloat16)
            product[where, :] = rounded.astype(jnp.float32)
            return past

        lax.fori_loop(0, steps // 2, multiply, past, unroll=4)

        rate = jnp.exp(-slope[:, lanes])
        powers[0] = rate
        leap = jnp.exp(slope[:, lanes] * float(-steps))
        for level in range(1, 4):
            powers[level] = leap
            leap = leap * leap
        rates = [wide_row(powers, (0, slice(m, m + 1))) for m in range(modes)]
        weights = [wide_row(weight, (slice(m, m + 1), lanes)) for m in range(modes)]

        def step(at, held):
            where = pl.ds(pl.multiple_of(at * SEGMENTS, SEGMENTS), SEGMENTS)
            value = product[where, :]
            held = tuple(rates[m] * held[m] + weights[m] * value for m in range(modes))
            local[where, lanes] = tree_sum(list(held))
            return held

        zero = jnp.zeros((SEGMENTS, LANES), jnp.float32)
        held = lax.fori_loop(0, steps, step, (zero,) * modes, unroll=4)
        for m in range(modes):
            leaps = [wide_row(powers, (1 + level, slice(m, m + 1))) for level in range(3)]
            total = jnp.where(place >= 1, pltpu.roll(held[m], 1, 0), 0.0)
            for level in range(3):
                reaching = 1 << level
                moved = leaps[level] * pltpu.roll(total, reaching, 0)
                total = total + jnp.where(place >= reaching, moved, 0.0)
            states[m, :, lanes] = total
            ended = leaps[0] * total + held[m]
            ends[0, m : m + 1, lanes] = ended[SEGMENTS - 1 :]


def exchange_kernel(
    count, tokens, ends, slope, entering, arrived, carries, send_out, recv_out, send_back, recv_back
):
    me = lax.axis_index("ctx")
    owners, modes, width = ends.shape
    greet("ctx", count, me)

    def out(slot, owner, k):
        return pltpu.make_async_remote_copy(
            src_ref=ends.at[owner],
            dst_ref=arrived.at[slot],
            send_sem=send_out.at[k],
            recv_sem=recv_out.at[slot],
            device_id={"ctx": owner},
            device_id_type=MESH,
        )

    def back(slot, peer, k):
        return pltpu.make_async_remote_copy(
            src_ref=carries.at[peer],
            dst_ref=entering.at[slot],
            send_sem=send_back.at[k],
            recv_sem=recv_back.at[slot],
            device_id={"ctx": peer},
            device_id_type=MESH,
        )

    for k in range(1, count):
        owner = lax.rem(me + k, count)

        @pl.when(owner < owners)
        def _():
            out(me, owner, k).start()

    @pl.when(me < owners)
    def _():
        arrived[me] = ends[me]
        lanes = pl.ds(pl.multiple_of(me * width, LANES), width)
        leap = jnp.exp(slope[:, lanes] * float(-tokens))
        for k in range(1, count):
            peer = lax.rem(me + k, count)
            out(peer, me, k).wait_recv()
        carry = jnp.zeros((modes, width), jnp.float32)
        for source in range(count):
            carries[source] = carry
            carry = leap * carry + arrived[source]
        for k in range(1, count):
            back(me, lax.rem(me + k, count), k).start()
        entering[me] = carries[me]

    for k in range(1, count):
        owner = lax.rem(me + k, count)

        @pl.when(owner < owners)
        def _():
            back(owner, me, k).wait_recv()
            out(me, owner, k).wait_send()

    @pl.when(me < owners)
    def _():
        for k in range(1, count):
            back(me, lax.rem(me + k, count), k).wait_send()


def third_kernel(keep, stream, inverse, feat, slope, local, states, entering, out, powers, result):
    width = stream.shape[1]
    steps = stream.shape[0] // SEGMENTS - keep
    modes = slope.shape[0]
    reach = feat.shape[0]
    place = lax.broadcasted_iota(jnp.int32, (SEGMENTS, LANES), 0)
    ahead = (place * -steps - 1).astype(jnp.float32)
    for block in range(width // LANES):
        lanes = slice(block * LANES, (block + 1) * LANES)
        taps = [wide_row(feat, (j, slice(0, 1), lanes)) for j in range(reach)]
        powers[...] = jnp.exp(-slope[:, lanes])
        rates = [wide_row(powers, (slice(m, m + 1),)) for m in range(modes)]

        def wide_pair(at):
            where = pl.ds(pl.multiple_of(at * SEGMENTS, 2 * SEGMENTS), 2 * SEGMENTS)
            both = stream[where, lanes].astype(jnp.float32)
            normed = both * inverse[where, :]
            halves = (slice(0, SEGMENTS), slice(SEGMENTS, 2 * SEGMENTS))
            return [(both[half], normed[half]) for half in halves]

        past = ()
        for at in range(keep - even(reach - 1), keep, 2):
            past = tuple(normed for _, normed in reversed(wide_pair(at))) + past
        past = past[: reach - 1]

        first = []
        for m in range(modes):
            reached = jnp.exp(wide_row(slope, (slice(m, m + 1), lanes)) * ahead)
            arriving = wide_row(entering, (0, slice(m, m + 1), lanes))
            first.append(rates[m] * states[m, :, lanes] + reached * arriving)

        def step(pair, carried):
            past, held = carried
            for half, (wide, normed) in enumerate(wide_pair(keep + 2 * pair)):
                at = 2 * pair + half
                series = (normed,) + past
                past = series[: reach - 1]
                where = pl.ds(pl.multiple_of(at * SEGMENTS, SEGMENTS), SEGMENTS)
                convolved = tree_sum(list(held)) + local[where, lanes]
                result[pl.ds(at, SEGMENTS, stride=steps), :] = wide + weighted(taps, series) * convolved
                held = tuple(rates[m] * held[m] for m in range(modes))
            return past, held

        lax.fori_loop(0, steps // 2, step, (past, tuple(first)), unroll=2)
        out[:, lanes] = result[...].astype(jnp.bfloat16)


def on_device(
    token_ids, embed_table, projected_table, feat_one, inner_taps, feat_two, decay, residue
):
    tokens = token_ids.shape[0]
    vocab, channels = embed_table.shape
    modes = decay.shape[1]
    count = lax.axis_size("ctx")
    peers = lax.axis_size("tp")
    steps = tokens // SEGMENTS
    keep = even(feat_two.shape[0] - 1)
    lead = even(keep + inner_taps.shape[0] - 1 + feat_one.shape[0] - 1)
    rows = (steps + keep) * SEGMENTS
    padded = -(-rows // LANES) * LANES
    plain = pltpu.CompilerParams(
        dimension_semantics=("arbitrary",), vmem_limit_bytes=VMEM_LIMIT
    )

    earlier = lax.ppermute(
        token_ids[tokens - HALO :], "ctx", [(source, source + 1) for source in range(count - 1)]
    )
    earlier = jnp.where(lax.axis_index("ctx") == 0, -1, earlier)
    ids = jnp.concatenate([earlier, token_ids])
    ids = jnp.stack(
        [ids[HALO - lead + s * steps : HALO + (s + 1) * steps] for s in range(SEGMENTS)], axis=1
    ).reshape(-1)
    one_hot = (ids[:, None] == jnp.arange(vocab, dtype=jnp.int32)[None, :]).astype(jnp.bfloat16)
    proj = jnp.transpose(projected_table, (1, 0, 2))

    wide = min(1024, channels)
    feat_spec = lambda size: pl.BlockSpec((feat_one.shape[0], 3, size), lambda c: (0, 0, c))
    stream, sums = pl.pallas_call(
        functools.partial(first_kernel, lead, keep),
        grid=(channels // wide,),
        in_specs=[
            pl.BlockSpec(one_hot.shape, lambda c: (0, 0)),
            pl.BlockSpec((vocab, wide), lambda c: (0, c)),
            pl.BlockSpec((3, vocab, wide), lambda c: (0, 0, c)),
            feat_spec(wide),
            pl.BlockSpec((inner_taps.shape[0], wide), lambda c: (0, c)),
        ],
        out_specs=[
            pl.BlockSpec((rows, wide), lambda c: (0, c)),
            pl.BlockSpec((SEGMENTS, padded), lambda c: (0, 0)),
        ],
        out_shape=[
            jax.ShapeDtypeStruct((rows, channels), jnp.bfloat16),
            jax.ShapeDtypeStruct((SEGMENTS, padded), jnp.float32),
        ],
        scratch_shapes=[
            pltpu.VMEM((4, one_hot.shape[0], LANES), jnp.float32),
            pltpu.VMEM((4, one_hot.shape[0], LANES), jnp.float32),
            pltpu.VMEM((padded, LANES), jnp.float32),
        ],
        compiler_params=plain,
        name="first_block",
    )(one_hot, embed_table, proj, feat_one, inner_taps)

    in_vmem = pl.BlockSpec(memory_space=pltpu.VMEM)
    inverse = pl.pallas_call(
        functools.partial(norm_kernel, peers, channels * peers),
        in_specs=[in_vmem],
        out_specs=in_vmem,
        out_shape=jax.ShapeDtypeStruct((padded, LANES), jnp.float32),
        scratch_shapes=[
            pltpu.VMEM((peers, SEGMENTS, padded), jnp.float32),
            pltpu.SemaphoreType.DMA((peers,)),
            pltpu.SemaphoreType.DMA((peers,)),
        ],
        compiler_params=pltpu.CompilerParams(
            collective_id=0, has_side_effects=True, vmem_limit_bytes=VMEM_LIMIT
        ),
        name="norm",
    )(sums)

    slope = jnp.transpose(decay)
    weight = jnp.transpose(residue)
    size = max(LANES, channels // count)
    owners = channels // size
    stream_spec = pl.BlockSpec((rows, size), lambda c: (0, c))
    inverse_spec = pl.BlockSpec((padded, LANES), lambda c: (0, 0))
    mode_spec = pl.BlockSpec((modes, size), lambda c: (0, c))
    token_spec = pl.BlockSpec((tokens, size), lambda c: (0, c))
    state_spec = pl.BlockSpec((modes, SEGMENTS, size), lambda c: (0, 0, c))
    whole_spec = pl.BlockSpec((1, modes, size), lambda c: (c, 0, 0))
    local, states, ends = pl.pallas_call(
        functools.partial(second_kernel, keep),
        grid=(owners,),
        in_specs=[stream_spec, inverse_spec, feat_spec(size), mode_spec, mode_spec],
        out_specs=[token_spec, state_spec, whole_spec],
        out_shape=[
            jax.ShapeDtypeStruct((tokens, channels), jnp.float32),
            jax.ShapeDtypeStruct((modes, SEGMENTS, channels), jnp.float32),
            jax.ShapeDtypeStruct((owners, modes, size), jnp.float32),
        ],
        scratch_shapes=[
            pltpu.VMEM((tokens, LANES), jnp.float32),
            pltpu.VMEM((4, modes, LANES), jnp.float32),
        ],
        compiler_params=plain,
        name="local_part",
    )(stream, inverse, feat_two, slope, weight)

    entering = pl.pallas_call(
        functools.partial(exchange_kernel, count, tokens),
        in_specs=[in_vmem, in_vmem],
        out_specs=in_vmem,
        out_shape=jax.ShapeDtypeStruct((owners, modes, size), jnp.float32),
        scratch_shapes=[
            pltpu.VMEM((count, modes, size), jnp.float32),
            pltpu.VMEM((count, modes, size), jnp.float32),
        ]
        + [pltpu.SemaphoreType.DMA((count,))] * 4,
        compiler_params=pltpu.CompilerParams(
            collective_id=1, has_side_effects=True, vmem_limit_bytes=VMEM_LIMIT
        ),
        name="exchange",
    )(ends, slope)

    return pl.pallas_call(
        functools.partial(third_kernel, keep),
        grid=(owners,),
        in_specs=[
            stream_spec,
            inverse_spec,
            feat_spec(size),
            mode_spec,
            token_spec,
            state_spec,
            whole_spec,
        ],
        out_specs=token_spec,
        out_shape=jax.ShapeDtypeStruct((tokens, channels), jnp.bfloat16),
        scratch_shapes=[
            pltpu.VMEM((modes, LANES), jnp.float32),
            pltpu.VMEM((tokens, LANES), jnp.float32),
        ],
        compiler_params=plain,
        name="long_convolution",
    )(stream, inverse, feat_two, slope, local, states, entering)


def solution(mesh):
    placed = (
        P("ctx"),
        P(None, "tp"),
        P(None, None, "tp"),
        P(None, None, "tp"),
        P(None, "tp"),
        P(None, None, "tp"),
        P("tp", None),
        P("tp", None),
    )
    return jax.shard_map(
        on_device, mesh=mesh, in_specs=placed, out_specs=P("ctx", "tp"), check_vma=False
    )
```

```python
import functools

import jax
import jax.numpy as jnp
from jax import lax
from jax.experimental import pallas as pl
from jax.experimental.pallas import tpu as pltpu
from jax.sharding import PartitionSpec as P

epsilon = 1e-06
HALO = 16
SEGMENTS = 8
LANES = 128
VMEM_LIMIT = 60 * 1024 * 1024
MESH = pl.DeviceIdType.MESH


def even(value):
    return value + value % 2


def wide_row(ref, index):
    return jnp.broadcast_to(ref[index], (SEGMENTS, LANES))


def weighted(taps, series):
    terms = [tap * value for tap, value in zip(taps, series)]
    total = terms[0]
    for term in terms[1:]:
        total = total + term
    return total


def tree_sum(terms):
    while len(terms) > 1:
        pairs = [a + b for a, b in zip(terms[::2], terms[1::2])]
        terms = pairs + terms[2 * len(pairs) :]
    return terms[0]


def first_kernel(lead, keep, one_hot, embed, proj, feat, inner, stream, sums, raw_a, raw_b, squares):
    blocks = embed.shape[1] // LANES
    steps = one_hot.shape[0] // SEGMENTS - lead
    reach = feat.shape[0]
    span = inner.shape[0]
    turn = pl.program_id(0)

    @pl.when(turn == 0)
    def _():
        squares[...] = jnp.zeros_like(squares)

    def project(raw):
        tables = [embed[...]] + [proj[s] for s in range(3)]
        both = jnp.dot(
            one_hot[...], jnp.concatenate(tables, axis=1), preferred_element_type=jnp.float32
        )
        for s in range(4):
            for block in range(blocks):
                at = (s * blocks + block) * LANES
                raw[s, block] = both[:, at : at + LANES]

    def mix(block, raw):
        lanes = slice(block * LANES, (block + 1) * LANES)
        feat_taps = [
            [wide_row(feat, (j, slice(s, s + 1), lanes)) for j in range(reach)] for s in range(3)
        ]
        inner_taps = [wide_row(inner, (slice(j, j + 1), lanes)) for j in range(span)]

        def row(s, step):
            return raw[s, block, pl.ds((step + lead) * SEGMENTS, SEGMENTS), :]

        mixed = []
        held = []
        pasts = [[], [], []]
        for step in range(-lead, steps):
            for s in range(3):
                if s == 0 and step < 1 - keep - reach:
                    continue
                pasts[s] = ([row(s + 1, step)] + pasts[s])[:reach]
            if step < reach - 1 - lead:
                continue
            keyed = weighted(feat_taps[1], pasts[1])
            valued = weighted(feat_taps[2], pasts[2])
            mixed = ([keyed * valued] + mixed)[:span]
            if step < -keep:
                continue
            queries = weighted(feat_taps[0], pasts[0])
            total = row(0, step) + queries * weighted(inner_taps, mixed)
            at = step + keep
            squares[pl.ds(at * SEGMENTS, SEGMENTS), :] += total * total
            held.append(total)
            if len(held) == 2:
                pair = jnp.concatenate(held, axis=0).astype(jnp.bfloat16)
                stream[pl.ds((at - 1) * SEGMENTS, 2 * SEGMENTS), lanes] = pair
                held = []

    def work(now, before):
        for block in range(blocks):
            mix(block, before)
        project(now)

    last = pl.num_programs(0) - 1

    @pl.when(turn == 0)
    def _():
        project(raw_a)

    @pl.when((turn > 0) & (turn % 2 == 1))
    def _():
        work(raw_b, raw_a)

    @pl.when((turn > 0) & (turn % 2 == 0))
    def _():
        work(raw_a, raw_b)

    @pl.when(turn == last)
    def _():
        sums[...] = lax.dot_general(
            jnp.ones((SEGMENTS, LANES), jnp.float32),
            squares[...],
            (((1,), (1,)), ((), ())),
            precision=lax.Precision.HIGHEST,
            preferred_element_type=jnp.float32,
        )


def norm_step(peers, channels, sums, inverse, parts, send, recv):
    me = lax.axis_index("tp")

    def copy(slot, peer):
        return pltpu.make_async_remote_copy(
            src_ref=sums,
            dst_ref=parts.at[slot],
            send_sem=send.at[peer],
            recv_sem=recv.at[slot],
            device_id={"tp": peer},
            device_id_type=MESH,
        )

    others = [lax.rem(me + k, peers) for k in range(1, peers)]
    for peer in others:
        copy(me, peer).start()
    parts[me] = sums[...]
    for peer in others:
        copy(peer, peer).wait_recv()
    total = parts[0]
    for k in range(1, peers):
        total = total + parts[k]
    row = lax.rsqrt(total / channels + epsilon)
    for at in range(0, inverse.shape[0], LANES):
        block = jnp.broadcast_to(row[0:1, at : at + LANES], (LANES, LANES))
        inverse[pl.ds(at, LANES), :] = jnp.transpose(block)
    for peer in others:
        copy(me, peer).wait_send()


def local_part(
    keep, block, at_lanes, stream, inverse, feat, slope, weight, local, states, ends, product, powers
):
    steps = stream.shape[0] // SEGMENTS - keep
    modes = slope.shape[0]
    reach = feat.shape[0]
    place = lax.broadcasted_iota(jnp.int32, (SEGMENTS, LANES), 0)
    lanes = slice(at_lanes * LANES, (at_lanes + 1) * LANES)
    taps = [[wide_row(feat, (j, slice(s, s + 1), lanes)) for j in range(reach)] for s in (1, 2)]

    def normed_pair(at):
        where = pl.ds(pl.multiple_of(at * SEGMENTS, 2 * SEGMENTS), 2 * SEGMENTS)
        both = stream[where, lanes].astype(jnp.float32) * inverse[where, :]
        return both[:SEGMENTS], both[SEGMENTS:]

    past = ()
    for at in range(keep - even(reach - 1), keep, 2):
        past = tuple(reversed(normed_pair(at))) + past
    past = past[: reach - 1]

    def multiply(pair, past):
        products = []
        for value in normed_pair(keep + 2 * pair):
            series = (value,) + past
            products.append(weighted(taps[0], series) * weighted(taps[1], series))
            past = series[: reach - 1]
        where = pl.ds(pl.multiple_of(pair * 2 * SEGMENTS, 2 * SEGMENTS), 2 * SEGMENTS)
        rounded = jnp.concatenate(products, axis=0).astype(jnp.bfloat16)
        product[where, :] = rounded.astype(jnp.float32)
        return past

    lax.fori_loop(0, steps // 2, multiply, past, unroll=8)

    powers[0] = jnp.exp(-slope[:, lanes])
    leap = jnp.exp(slope[:, lanes] * float(-steps))
    for level in range(1, 4):
        powers[level] = leap
        leap = leap * leap
    rates = [wide_row(powers, (0, slice(m, m + 1))) for m in range(modes)]
    weights = [wide_row(weight, (slice(m, m + 1), lanes)) for m in range(modes)]

    def step(at, held):
        where = pl.ds(pl.multiple_of(at * SEGMENTS, SEGMENTS), SEGMENTS)
        value = product[where, :]
        held = tuple(rates[m] * held[m] + weights[m] * value for m in range(modes))
        local[block, at_lanes, where, :] = tree_sum(list(held))
        return held

    zero = jnp.zeros((SEGMENTS, LANES), jnp.float32)
    held = lax.fori_loop(0, steps, step, (zero,) * modes, unroll=8)
    for m in range(modes):
        leaps = [wide_row(powers, (1 + level, slice(m, m + 1))) for level in range(3)]
        total = jnp.where(place >= 1, pltpu.roll(held[m], 1, 0), 0.0)
        for level in range(3):
            reaching = 1 << level
            moved = leaps[level] * pltpu.roll(total, reaching, 0)
            total = total + jnp.where(place >= reaching, moved, 0.0)
        states[block, at_lanes, m] = total
        ended = leaps[0] * total + held[m]
        ends[block, m : m + 1, lanes] = ended[SEGMENTS - 1 :]


def whole_part(
    keep, block, at_lanes, stream, inverse, feat, slope, local, states, entering, out, powers, result
):
    steps = stream.shape[0] // SEGMENTS - keep
    modes = slope.shape[0]
    reach = feat.shape[0]
    place = lax.broadcasted_iota(jnp.int32, (SEGMENTS, LANES), 0)
    ahead = (place * -steps - 1).astype(jnp.float32)
    lanes = slice(at_lanes * LANES, (at_lanes + 1) * LANES)
    taps = [wide_row(feat, (j, slice(0, 1), lanes)) for j in range(reach)]
    powers[0] = jnp.exp(-slope[:, lanes])
    rates = [wide_row(powers, (0, slice(m, m + 1))) for m in range(modes)]

    def wide_pair(at):
        where = pl.ds(pl.multiple_of(at * SEGMENTS, 2 * SEGMENTS), 2 * SEGMENTS)
        both = stream[where, lanes].astype(jnp.float32)
        normed = both * inverse[where, :]
        halves = (slice(0, SEGMENTS), slice(SEGMENTS, 2 * SEGMENTS))
        return [(both[half], normed[half]) for half in halves]

    past = ()
    for at in range(keep - even(reach - 1), keep, 2):
        past = tuple(normed for _, normed in reversed(wide_pair(at))) + past
    past = past[: reach - 1]

    first = []
    for m in range(modes):
        reached = jnp.exp(wide_row(slope, (slice(m, m + 1), lanes)) * ahead)
        arriving = wide_row(entering, (block, slice(m, m + 1), lanes))
        first.append(rates[m] * states[block, at_lanes, m] + reached * arriving)

    def step(pair, carried):
        past, held = carried
        for half, (wide, normed) in enumerate(wide_pair(keep + 2 * pair)):
            at = 2 * pair + half
            series = (normed,) + past
            past = series[: reach - 1]
            where = pl.ds(pl.multiple_of(at * SEGMENTS, SEGMENTS), SEGMENTS)
            convolved = tree_sum(list(held)) + local[block, at_lanes, where, :]
            result[pl.ds(at, SEGMENTS, stride=steps), :] = wide + weighted(taps, series) * convolved
            held = tuple(rates[m] * held[m] for m in range(modes))
        return past, held

    lax.fori_loop(0, steps // 2, step, (past, tuple(first)), unroll=4)
    out[:, lanes] = result[...].astype(jnp.bfloat16)


def second_kernel(
    keep,
    count,
    peers,
    all_channels,
    sums,
    slope_all,
    stream,
    feat,
    slope,
    weight,
    out,
    inverse,
    parts,
    local,
    states,
    ends,
    arrived,
    carries,
    entering,
    product,
    powers,
    result,
    send_norm,
    recv_norm,
    send_out,
    recv_out,
    send_back,
    recv_back,
):
    turn = pl.program_id(0)
    me = lax.axis_index("ctx")
    owners, modes, width = ends.shape
    tokens = out.shape[0]
    blocks = width // LANES
    others = [lax.rem(me + k, count) for k in range(1, count)]

    def to_owner(slot, owner):
        return pltpu.make_async_remote_copy(
            src_ref=ends.at[owner],
            dst_ref=arrived.at[slot],
            send_sem=send_out.at[owner],
            recv_sem=recv_out.at[slot],
            device_id={"ctx": owner},
            device_id_type=MESH,
        )

    def from_owner(slot, peer):
        return pltpu.make_async_remote_copy(
            src_ref=carries.at[peer],
            dst_ref=entering.at[slot],
            send_sem=send_back.at[peer],
            recv_sem=recv_back.at[slot],
            device_id={"ctx": peer},
            device_id_type=MESH,
        )

    @pl.when(turn == 0)
    def _():
        barrier = pltpu.get_barrier_semaphore()
        for peer in others:
            pl.semaphore_signal(barrier, inc=1, device_id={"ctx": peer}, device_id_type=MESH)
        mine = lax.axis_index("tp")
        for k in range(1, peers):
            peer = lax.rem(mine + k, peers)
            pl.semaphore_signal(barrier, inc=1, device_id={"tp": peer}, device_id_type=MESH)
        pl.semaphore_wait(barrier, count - 1 + peers - 1)
        norm_step(peers, all_channels, sums, inverse, parts, send_norm, recv_norm)

    @pl.when((turn == me + min(2, owners)) & (me < owners))
    def _():
        lanes = pl.ds(pl.multiple_of(me * width, LANES), width)
        leap = jnp.exp(slope_all[:, lanes] * float(-tokens))
        arrived[me] = ends[me]
        for peer in others:
            to_owner(peer, me).wait_recv()
        carry = jnp.zeros((modes, width), jnp.float32)
        for source in range(count):
            carries[source] = carry
            carry = leap * carry + arrived[source]
        for peer in others:
            from_owner(me, peer).start()
        entering[me] = carries[me]

    @pl.when(turn < owners)
    def _():
        for at in range(blocks):
            local_part(
                keep, turn, at, stream, inverse, feat, slope, weight, local, states, ends, product, powers
            )

        @pl.when(turn != me)
        def _():
            to_owner(me, turn).start()

    @pl.when(turn >= owners)
    def _():
        block = turn - owners

        @pl.when(block != me)
        def _():
            from_owner(block, me).wait_recv()

        for at in range(blocks):
            whole_part(
                keep, block, at, stream, inverse, feat, slope, local, states, entering, out, powers, result
            )

    @pl.when(turn == 2 * owners - 1)
    def _():
        for peer in others:

            @pl.when(peer < owners)
            def _():
                to_owner(me, peer).wait_send()

        @pl.when(me < owners)
        def _():
            for peer in others:
                from_owner(me, peer).wait_send()


def on_device(
    token_ids, embed_table, projected_table, feat_one, inner_taps, feat_two, decay, residue
):
    tokens = token_ids.shape[0]
    vocab, channels = embed_table.shape
    modes = decay.shape[1]
    count = lax.axis_size("ctx")
    peers = lax.axis_size("tp")
    steps = tokens // SEGMENTS
    keep = even(feat_two.shape[0] - 1)
    lead = even(keep + inner_taps.shape[0] - 1 + feat_one.shape[0] - 1)
    rows = (steps + keep) * SEGMENTS
    padded = -(-rows // LANES) * LANES
    earlier = lax.ppermute(
        token_ids[tokens - HALO :], "ctx", [(source, source + 1) for source in range(count - 1)]
    )
    earlier = jnp.where(lax.axis_index("ctx") == 0, -1, earlier)
    ids = jnp.concatenate([earlier, token_ids])
    ids = jnp.stack(
        [ids[HALO - lead + s * steps : HALO + (s + 1) * steps] for s in range(SEGMENTS)], axis=1
    ).reshape(-1)
    one_hot = (ids[:, None] == jnp.arange(vocab, dtype=jnp.int32)[None, :]).astype(jnp.bfloat16)
    proj = jnp.transpose(projected_table, (1, 0, 2))

    wide = min(256, channels)
    blocks = channels // wide
    lagging = lambda c: jnp.maximum(c - 1, 0)
    ahead = lambda c: jnp.minimum(c, blocks - 1)
    raw = pltpu.VMEM((4, wide // LANES, one_hot.shape[0], LANES), jnp.float32)
    stream, sums = pl.pallas_call(
        functools.partial(first_kernel, lead, keep),
        grid=(blocks + 1,),
        in_specs=[
            pl.BlockSpec(one_hot.shape, lambda c: (0, 0)),
            pl.BlockSpec((vocab, wide), lambda c: (0, ahead(c))),
            pl.BlockSpec((3, vocab, wide), lambda c: (0, 0, ahead(c))),
            pl.BlockSpec((feat_one.shape[0], 3, wide), lambda c: (0, 0, lagging(c))),
            pl.BlockSpec((inner_taps.shape[0], wide), lambda c: (0, lagging(c))),
        ],
        out_specs=[
            pl.BlockSpec((rows, wide), lambda c: (0, lagging(c))),
            pl.BlockSpec((SEGMENTS, padded), lambda c: (0, 0)),
        ],
        out_shape=[
            jax.ShapeDtypeStruct((rows, channels), jnp.bfloat16),
            jax.ShapeDtypeStruct((SEGMENTS, padded), jnp.float32),
        ],
        scratch_shapes=[raw, raw, pltpu.VMEM((padded, LANES), jnp.float32)],
        compiler_params=pltpu.CompilerParams(
            dimension_semantics=("arbitrary",), vmem_limit_bytes=VMEM_LIMIT
        ),
        name="first_block",
    )(one_hot, embed_table, proj, feat_one, inner_taps)

    slope = jnp.transpose(decay)
    weight = jnp.transpose(residue)
    size = max(LANES, channels // count)
    owners = channels // size
    turning = lambda c: lax.rem(c, owners)
    mode_spec = pl.BlockSpec((modes, size), lambda c: (0, turning(c)))
    shared = lambda number: pltpu.VMEM((number, modes, size), jnp.float32)
    return pl.pallas_call(
        functools.partial(second_kernel, keep, count, peers, channels * peers),
        grid=(2 * owners,),
        in_specs=[
            pl.BlockSpec((SEGMENTS, padded), lambda c: (0, 0)),
            pl.BlockSpec((modes, channels), lambda c: (0, 0)),
            pl.BlockSpec((rows, size), lambda c: (0, turning(c))),
            pl.BlockSpec((feat_two.shape[0], 3, size), lambda c: (0, 0, turning(c))),
            mode_spec,
            mode_spec,
        ],
        out_specs=pl.BlockSpec((tokens, size), lambda c: (0, jnp.maximum(c - owners, 0))),
        out_shape=jax.ShapeDtypeStruct((tokens, channels), jnp.bfloat16),
        scratch_shapes=[
            pltpu.VMEM((padded, LANES), jnp.float32),
            pltpu.VMEM((peers, SEGMENTS, padded), jnp.float32),
            pltpu.VMEM((owners, size // LANES, tokens, LANES), jnp.float32),
            pltpu.VMEM((owners, size // LANES, modes, SEGMENTS, LANES), jnp.float32),
            shared(owners),
            shared(count),
            shared(count),
            shared(owners),
            pltpu.VMEM((tokens, LANES), jnp.float32),
            pltpu.VMEM((4, modes, LANES), jnp.float32),
            pltpu.VMEM((tokens, LANES), jnp.float32),
            pltpu.SemaphoreType.DMA((peers,)),
            pltpu.SemaphoreType.DMA((peers,)),
        ]
        + [pltpu.SemaphoreType.DMA((count,))] * 4,
        compiler_params=pltpu.CompilerParams(
            dimension_semantics=("arbitrary",),
            collective_id=0,
            has_side_effects=True,
            vmem_limit_bytes=VMEM_LIMIT,
        ),
        name="long_convolution",
    )(sums, slope, stream, feat_two, slope, weight)


def solution(mesh):
    placed = (
        P("ctx"),
        P(None, "tp"),
        P(None, None, "tp"),
        P(None, None, "tp"),
        P(None, "tp"),
        P(None, None, "tp"),
        P("tp", None),
        P("tp", None),
    )
    return jax.shard_map(
        on_device, mesh=mesh, in_specs=placed, out_specs=P("ctx", "tp"), check_vma=False
    )
```

```python
import functools

import jax
import jax.numpy as jnp
from jax import lax
from jax.experimental import pallas as pl
from jax.experimental.pallas import tpu as pltpu
from jax.sharding import PartitionSpec as P

epsilon = 1e-06
HALO = 16
SEGMENTS = 8
LANES = 128
VMEM_LIMIT = 60 * 1024 * 1024
MESH = pl.DeviceIdType.MESH


def even(value):
    return value + value % 2


def wide_row(ref, index):
    return jnp.broadcast_to(ref[index], (SEGMENTS, LANES))


def lanes_of(block):
    return pl.ds(pl.multiple_of(block * LANES, LANES), LANES)


def weighted(taps, series):
    terms = [tap * value for tap, value in zip(taps, series)]
    total = terms[0]
    for term in terms[1:]:
        total = total + term
    return total


def tree_sum(terms):
    while len(terms) > 1:
        pairs = [a + b for a, b in zip(terms[::2], terms[1::2])]
        terms = pairs + terms[2 * len(pairs) :]
    return terms[0]


def first_kernel(
    lead,
    keep,
    earlier,
    ids,
    embed,
    proj,
    feat,
    inner,
    stream,
    sums,
    raw_a,
    raw_b,
    squares,
    natural,
    one_hot,
    tables,
    arrival,
):
    turn = pl.program_id(0)
    groups, _, vocab, width = tables.shape
    blocks = width // LANES
    tokens = ids.shape[1]
    steps = tokens // SEGMENTS
    reach = feat.shape[0]
    span = inner.shape[0]

    def fetches(group):
        lanes = pl.ds(pl.multiple_of(group * width, LANES), width)
        return (
            pltpu.make_async_copy(
                embed.at[:, lanes], tables.at[group, 0], arrival.at[group, 0]
            ),
            pltpu.make_async_copy(
                proj.at[:, :, lanes], tables.at[group, pl.ds(1, 3)], arrival.at[group, 1]
            ),
        )

    def set_up():
        for group in range(groups):
            for fetch in fetches(group):
                fetch.start()
        squares[...] = jnp.zeros_like(squares)
        pieces = [earlier[:, tokens - LANES :]]
        pieces += [ids[:, at : at + LANES] for at in range(0, tokens, LANES)]
        for at, piece in enumerate(pieces):
            square = jnp.broadcast_to(piece.astype(jnp.float32), (LANES, LANES))
            natural[pl.ds(at * LANES, LANES), :] = jnp.transpose(square)
        entry = lax.broadcasted_iota(jnp.int32, (2 * SEGMENTS, LANES), 1)
        for step in range(-lead, steps, 2):
            rows = [natural[pl.ds(LANES + step + k, SEGMENTS, stride=steps), :] for k in range(2)]
            found = jnp.concatenate(rows, axis=0)
            for at in range(0, vocab, LANES):
                equal = found == (entry + at).astype(jnp.float32)
                one_hot[pl.ds((step + lead) * SEGMENTS, 2 * SEGMENTS), at : at + LANES] = jnp.where(
                    equal, 1.0, 0.0
                ).astype(jnp.bfloat16)

    def project(raw):
        both = jnp.dot(
            one_hot[...],
            jnp.concatenate([tables[turn, s] for s in range(4)], axis=1),
            preferred_element_type=jnp.float32,
        )
        for s in range(4):
            for block in range(blocks):
                at = (s * blocks + block) * LANES
                raw[s, block] = both[:, at : at + LANES]

    def mix(block, raw):
        lanes = slice(block * LANES, (block + 1) * LANES)
        here = lanes_of((turn - 1) * blocks + block)
        feat_taps = [
            [wide_row(feat, (j, slice(s, s + 1), here)) for j in range(reach)] for s in range(3)
        ]
        inner_taps = [wide_row(inner, (slice(j, j + 1), here)) for j in range(span)]

        def row(s, step):
            return raw[s, block, pl.ds((step + lead) * SEGMENTS, SEGMENTS), :]

        mixed = []
        held = []
        pasts = [[], [], []]
        for step in range(-lead, steps):
            for s in range(3):
                if s == 0 and step < 1 - keep - reach:
                    continue
                pasts[s] = ([row(s + 1, step)] + pasts[s])[:reach]
            if step < reach - 1 - lead:
                continue
            keyed = weighted(feat_taps[1], pasts[1])
            valued = weighted(feat_taps[2], pasts[2])
            mixed = ([keyed * valued] + mixed)[:span]
            if step < -keep:
                continue
            queries = weighted(feat_taps[0], pasts[0])
            total = row(0, step) + queries * weighted(inner_taps, mixed)
            at = step + keep
            squares[pl.ds(at * SEGMENTS, SEGMENTS), :] += total * total
            held.append(total)
            if len(held) == 2:
                pair = jnp.concatenate(held, axis=0).astype(jnp.bfloat16)
                stream[pl.ds((at - 1) * SEGMENTS, 2 * SEGMENTS), lanes] = pair
                held = []

    raws = (raw_a, raw_b)

    def mix_all(raw):
        for block in range(blocks):
            mix(block, raw)

    def work(parity):
        for fetch in fetches(turn):
            fetch.wait()
        mix_all(raws[1 - parity])
        project(raws[parity])

    @pl.when(turn == 0)
    def _():
        set_up()
        for fetch in fetches(0):
            fetch.wait()
        project(raw_a)

    for parity in range(2):

        @pl.when((turn > 0) & (turn < groups) & (turn % 2 == parity))
        def _():
            work(parity)

    @pl.when(turn == groups)
    def _():
        mix_all(raws[(groups - 1) % 2])
        sums[...] = lax.dot_general(
            jnp.ones((SEGMENTS, LANES), jnp.float32),
            squares[...],
            (((1,), (1,)), ((), ())),
            precision=lax.Precision.HIGHEST,
            preferred_element_type=jnp.float32,
        )


def norm_step(peers, channels, sums, inverse, parts, send, recv):
    me = lax.axis_index("tp")

    def copy(slot, peer):
        return pltpu.make_async_remote_copy(
            src_ref=sums,
            dst_ref=parts.at[slot],
            send_sem=send.at[peer],
            recv_sem=recv.at[slot],
            device_id={"tp": peer},
            device_id_type=MESH,
        )

    others = [lax.rem(me + k, peers) for k in range(1, peers)]
    for peer in others:
        copy(me, peer).start()
    parts[me] = sums[...]
    for peer in others:
        copy(peer, peer).wait_recv()
    total = parts[0]
    for k in range(1, peers):
        total = total + parts[k]
    row = lax.rsqrt(total / channels + epsilon)
    for at in range(0, inverse.shape[0], LANES):
        block = jnp.broadcast_to(row[0:1, at : at + LANES], (LANES, LANES))
        inverse[pl.ds(at, LANES), :] = jnp.transpose(block)
    for peer in others:
        copy(me, peer).wait_send()


def local_part(
    keep, block, at_lanes, stream, inverse, feat, slope, weight, local, states, ends, product, powers
):
    steps = stream.shape[0] // SEGMENTS - keep
    modes = slope.shape[0]
    reach = feat.shape[0]
    place = lax.broadcasted_iota(jnp.int32, (SEGMENTS, LANES), 0)
    lanes = slice(at_lanes * LANES, (at_lanes + 1) * LANES)
    here = lanes_of(block * (stream.shape[1] // LANES) + at_lanes)
    taps = [[wide_row(feat, (j, slice(s, s + 1), here)) for j in range(reach)] for s in (1, 2)]

    def normed_pair(at):
        where = pl.ds(pl.multiple_of(at * SEGMENTS, 2 * SEGMENTS), 2 * SEGMENTS)
        both = stream[where, lanes].astype(jnp.float32) * inverse[where, :]
        return both[:SEGMENTS], both[SEGMENTS:]

    past = ()
    for at in range(keep - even(reach - 1), keep, 2):
        past = tuple(reversed(normed_pair(at))) + past
    past = past[: reach - 1]

    def multiply(pair, past):
        products = []
        for value in normed_pair(keep + 2 * pair):
            series = (value,) + past
            products.append(weighted(taps[0], series) * weighted(taps[1], series))
            past = series[: reach - 1]
        where = pl.ds(pl.multiple_of(pair * 2 * SEGMENTS, 2 * SEGMENTS), 2 * SEGMENTS)
        rounded = jnp.concatenate(products, axis=0).astype(jnp.bfloat16)
        product[where, :] = rounded.astype(jnp.float32)
        return past

    lax.fori_loop(0, steps // 2, multiply, past, unroll=16)

    powers[0] = jnp.exp(-slope[:, here])
    leap = jnp.exp(slope[:, here] * float(-steps))
    for level in range(1, 4):
        powers[level] = leap
        leap = leap * leap
    rates = [wide_row(powers, (0, slice(m, m + 1))) for m in range(modes)]
    weights = [wide_row(weight, (slice(m, m + 1), here)) for m in range(modes)]

    def step(at, held):
        where = pl.ds(pl.multiple_of(at * SEGMENTS, SEGMENTS), SEGMENTS)
        value = product[where, :]
        held = tuple(rates[m] * held[m] + weights[m] * value for m in range(modes))
        local[block, at_lanes, where, :] = tree_sum(list(held))
        return held

    zero = jnp.zeros((SEGMENTS, LANES), jnp.float32)
    held = lax.fori_loop(0, steps, step, (zero,) * modes, unroll=16)
    for m in range(modes):
        leaps = [wide_row(powers, (1 + level, slice(m, m + 1))) for level in range(3)]
        total = jnp.where(place >= 1, pltpu.roll(held[m], 1, 0), 0.0)
        for level in range(3):
            reaching = 1 << level
            moved = leaps[level] * pltpu.roll(total, reaching, 0)
            total = total + jnp.where(place >= reaching, moved, 0.0)
        states[block, at_lanes, m] = total
        ended = leaps[0] * total + held[m]
        ends[block, m : m + 1, lanes] = ended[SEGMENTS - 1 :]


def whole_part(
    keep, block, at_lanes, stream, inverse, feat, slope, local, states, entering, out, powers, result
):
    steps = stream.shape[0] // SEGMENTS - keep
    modes = slope.shape[0]
    reach = feat.shape[0]
    place = lax.broadcasted_iota(jnp.int32, (SEGMENTS, LANES), 0)
    ahead = (place * -steps - 1).astype(jnp.float32)
    lanes = slice(at_lanes * LANES, (at_lanes + 1) * LANES)
    here = lanes_of(block * (stream.shape[1] // LANES) + at_lanes)
    taps = [wide_row(feat, (j, slice(0, 1), here)) for j in range(reach)]
    powers[0] = jnp.exp(-slope[:, here])
    rates = [wide_row(powers, (0, slice(m, m + 1))) for m in range(modes)]

    def wide_pair(at):
        where = pl.ds(pl.multiple_of(at * SEGMENTS, 2 * SEGMENTS), 2 * SEGMENTS)
        both = stream[where, lanes].astype(jnp.float32)
        normed = both * inverse[where, :]
        halves = (slice(0, SEGMENTS), slice(SEGMENTS, 2 * SEGMENTS))
        return [(both[half], normed[half]) for half in halves]

    past = ()
    for at in range(keep - even(reach - 1), keep, 2):
        past = tuple(normed for _, normed in reversed(wide_pair(at))) + past
    past = past[: reach - 1]

    first = []
    for m in range(modes):
        reached = jnp.exp(wide_row(slope, (slice(m, m + 1), here)) * ahead)
        arriving = wide_row(entering, (block, slice(m, m + 1), lanes))
        first.append(rates[m] * states[block, at_lanes, m] + reached * arriving)

    def step(pair, carried):
        past, held = carried
        for half, (wide, normed) in enumerate(wide_pair(keep + 2 * pair)):
            at = 2 * pair + half
            series = (normed,) + past
            past = series[: reach - 1]
            where = pl.ds(pl.multiple_of(at * SEGMENTS, SEGMENTS), SEGMENTS)
            convolved = tree_sum(list(held)) + local[block, at_lanes, where, :]
            result[pl.ds(at, SEGMENTS, stride=steps), :] = wide + weighted(taps, series) * convolved
            held = tuple(rates[m] * held[m] for m in range(modes))
        return past, held

    lax.fori_loop(0, steps // 2, step, (past, tuple(first)), unroll=8)
    out[:, lanes] = result[...].astype(jnp.bfloat16)


def second_kernel(
    keep,
    count,
    peers,
    all_channels,
    sums,
    stream,
    feat,
    slope,
    weight,
    out,
    inverse,
    parts,
    local,
    states,
    ends,
    arrived,
    carries,
    entering,
    product,
    powers,
    result,
    send_norm,
    recv_norm,
    send_out,
    recv_out,
    send_back,
    recv_back,
):
    turn = pl.program_id(0)
    me = lax.axis_index("ctx")
    owners, modes, width = ends.shape
    tokens = out.shape[0]
    blocks = width // LANES
    others = [lax.rem(me + k, count) for k in range(1, count)]

    def to_owner(slot, owner):
        return pltpu.make_async_remote_copy(
            src_ref=ends.at[owner],
            dst_ref=arrived.at[slot],
            send_sem=send_out.at[owner],
            recv_sem=recv_out.at[slot],
            device_id={"ctx": owner},
            device_id_type=MESH,
        )

    def from_owner(slot, peer):
        return pltpu.make_async_remote_copy(
            src_ref=carries.at[peer],
            dst_ref=entering.at[slot],
            send_sem=send_back.at[peer],
            recv_sem=recv_back.at[slot],
            device_id={"ctx": peer},
            device_id_type=MESH,
        )

    @pl.when(turn == 0)
    def _():
        barrier = pltpu.get_barrier_semaphore()
        for peer in others:
            pl.semaphore_signal(barrier, inc=1, device_id={"ctx": peer}, device_id_type=MESH)
        mine = lax.axis_index("tp")
        for k in range(1, peers):
            peer = lax.rem(mine + k, peers)
            pl.semaphore_signal(barrier, inc=1, device_id={"tp": peer}, device_id_type=MESH)
        pl.semaphore_wait(barrier, count - 1 + peers - 1)
        norm_step(peers, all_channels, sums, inverse, parts, send_norm, recv_norm)

    @pl.when((turn == me + owners // 2) & (me < owners))
    def _():
        lanes = pl.ds(pl.multiple_of(me * width, LANES), width)
        leap = jnp.exp(slope[:, lanes] * float(-tokens))
        arrived[me] = ends[me]
        for peer in others:
            to_owner(peer, me).wait_recv()
        carry = jnp.zeros((modes, width), jnp.float32)
        for source in range(count):
            carries[source] = carry
            carry = leap * carry + arrived[source]
        for peer in others:
            from_owner(me, peer).start()
        entering[me] = carries[me]

    @pl.when(turn < owners)
    def _():
        for at in range(blocks):
            local_part(
                keep, turn, at, stream, inverse, feat, slope, weight, local, states, ends, product, powers
            )

        @pl.when(turn != me)
        def _():
            to_owner(me, turn).start()

    @pl.when(turn >= owners)
    def _():
        block = turn - owners

        @pl.when(block != me)
        def _():
            from_owner(block, me).wait_recv()

        for at in range(blocks):
            whole_part(
                keep, block, at, stream, inverse, feat, slope, local, states, entering, out, powers, result
            )

    @pl.when(turn == 2 * owners - 1)
    def _():
        for peer in others:

            @pl.when(peer < owners)
            def _():
                to_owner(me, peer).wait_send()

        @pl.when(me < owners)
        def _():
            for peer in others:
                from_owner(me, peer).wait_send()


def on_device(
    token_ids, embed_table, projected_table, feat_one, inner_taps, feat_two, decay, residue
):
    tokens = token_ids.shape[0]
    vocab, channels = embed_table.shape
    modes = decay.shape[1]
    count = lax.axis_size("ctx")
    peers = lax.axis_size("tp")
    steps = tokens // SEGMENTS
    keep = even(feat_two.shape[0] - 1)
    lead = even(keep + inner_taps.shape[0] - 1 + feat_one.shape[0] - 1)
    rows = (steps + keep) * SEGMENTS
    padded = -(-rows // LANES) * LANES
    earlier = lax.ppermute(token_ids, "ctx", [(source, source + 1) for source in range(count - 1)])
    earlier = jnp.where(lax.axis_index("ctx") == 0, -1, earlier)
    proj = jnp.transpose(projected_table, (1, 0, 2))

    wide = min(256, channels)
    blocks = channels // wide
    lagging = lambda c: jnp.maximum(c - 1, 0)
    extended = (steps + lead) * SEGMENTS
    raw = pltpu.VMEM((4, wide // LANES, extended, LANES), jnp.float32)
    row_spec = pl.BlockSpec((1, tokens), lambda c: (0, 0))
    stream, sums = pl.pallas_call(
        functools.partial(first_kernel, lead, keep),
        grid=(blocks + 1,),
        in_specs=[
            row_spec,
            row_spec,
            pl.BlockSpec(memory_space=pl.ANY),
            pl.BlockSpec(memory_space=pl.ANY),
            pl.BlockSpec(feat_one.shape, lambda c: (0, 0, 0)),
            pl.BlockSpec(inner_taps.shape, lambda c: (0, 0)),
        ],
        out_specs=[
            pl.BlockSpec((rows, wide), lambda c: (0, lagging(c))),
            pl.BlockSpec((SEGMENTS, padded), lambda c: (0, 0)),
        ],
        out_shape=[
            jax.ShapeDtypeStruct((rows, channels), jnp.bfloat16),
            jax.ShapeDtypeStruct((SEGMENTS, padded), jnp.float32),
        ],
        scratch_shapes=[
            raw,
            raw,
            pltpu.VMEM((padded, LANES), jnp.float32),
            pltpu.VMEM((LANES + tokens, LANES), jnp.float32),
            pltpu.VMEM((extended, vocab), jnp.bfloat16),
            pltpu.VMEM((blocks, 4, vocab, wide), jnp.bfloat16),
            pltpu.SemaphoreType.DMA((blocks, 2)),
        ],
        compiler_params=pltpu.CompilerParams(
            dimension_semantics=("arbitrary",), vmem_limit_bytes=VMEM_LIMIT
        ),
        name="first_block",
    )(earlier[None], token_ids[None], embed_table, proj, feat_one, inner_taps)

    slope = jnp.transpose(decay)
    weight = jnp.transpose(residue)
    size = max(LANES, channels // count)
    owners = channels // size
    turning = lambda c: lax.rem(c, owners)
    mode_spec = pl.BlockSpec((modes, channels), lambda c: (0, 0))
    shared = lambda number: pltpu.VMEM((number, modes, size), jnp.float32)
    return pl.pallas_call(
        functools.partial(second_kernel, keep, count, peers, channels * peers),
        grid=(2 * owners,),
        in_specs=[
            pl.BlockSpec((SEGMENTS, padded), lambda c: (0, 0)),
            pl.BlockSpec((rows, size), lambda c: (0, turning(c))),
            pl.BlockSpec(feat_two.shape, lambda c: (0, 0, 0)),
            mode_spec,
            mode_spec,
        ],
        out_specs=pl.BlockSpec((tokens, size), lambda c: (0, jnp.maximum(c - owners, 0))),
        out_shape=jax.ShapeDtypeStruct((tokens, channels), jnp.bfloat16),
        scratch_shapes=[
            pltpu.VMEM((padded, LANES), jnp.float32),
            pltpu.VMEM((peers, SEGMENTS, padded), jnp.float32),
            pltpu.VMEM((owners, size // LANES, tokens, LANES), jnp.float32),
            pltpu.VMEM((owners, size // LANES, modes, SEGMENTS, LANES), jnp.float32),
            shared(owners),
            shared(count),
            shared(count),
            shared(owners),
            pltpu.VMEM((tokens, LANES), jnp.float32),
            pltpu.VMEM((4, modes, LANES), jnp.float32),
            pltpu.VMEM((tokens, LANES), jnp.float32),
            pltpu.SemaphoreType.DMA((peers,)),
            pltpu.SemaphoreType.DMA((peers,)),
        ]
        + [pltpu.SemaphoreType.DMA((count,))] * 4,
        compiler_params=pltpu.CompilerParams(
            dimension_semantics=("arbitrary",),
            collective_id=0,
            has_side_effects=True,
            vmem_limit_bytes=VMEM_LIMIT,
        ),
        name="long_convolution",
    )(sums, stream, feat_two, slope, weight)


def solution(mesh):
    placed = (
        P("ctx"),
        P(None, "tp"),
        P(None, None, "tp"),
        P(None, None, "tp"),
        P(None, "tp"),
        P(None, None, "tp"),
        P("tp", None),
        P("tp", None),
    )
    return jax.shard_map(
        on_device, mesh=mesh, in_specs=placed, out_specs=P("ctx", "tp"), check_vma=False
    )
```

```python
import functools

import jax
import jax.numpy as jnp
from jax import lax
from jax.experimental import pallas as pl
from jax.experimental.pallas import tpu as pltpu
from jax.sharding import PartitionSpec as P

epsilon = 1e-06
HALO = 16
SEGMENTS = 8
LANES = 128
VMEM_LIMIT = 60 * 1024 * 1024
MESH = pl.DeviceIdType.MESH


def even(value):
    return value + value % 2


def wide_row(ref, index):
    return jnp.broadcast_to(ref[index], (SEGMENTS, LANES))


def lanes_of(block):
    return pl.ds(pl.multiple_of(block * LANES, LANES), LANES)


def weighted(taps, series):
    terms = [tap * value for tap, value in zip(taps, series)]
    total = terms[0]
    for term in terms[1:]:
        total = total + term
    return total


def tree_sum(terms):
    while len(terms) > 1:
        pairs = [a + b for a, b in zip(terms[::2], terms[1::2])]
        terms = pairs + terms[2 * len(pairs) :]
    return terms[0]


def first_part(
    turn,
    lead,
    keep,
    get_earlier,
    earlier,
    ids,
    embed,
    proj,
    feat,
    inner,
    stream,
    sums,
    raw_a,
    raw_b,
    squares,
    natural,
    one_hot,
    tables,
    arrival,
):
    groups, _, vocab, width = tables.shape
    blocks = width // LANES
    tokens = ids.shape[1]
    steps = tokens // SEGMENTS
    reach = feat.shape[0]
    span = inner.shape[0]

    def fetches(group):
        lanes = pl.ds(pl.multiple_of(group * width, LANES), width)
        return (
            pltpu.make_async_copy(
                embed.at[:, lanes], tables.at[group, 0], arrival.at[group, 0]
            ),
            pltpu.make_async_copy(
                proj.at[:, :, lanes], tables.at[group, pl.ds(1, 3)], arrival.at[group, 1]
            ),
        )

    def set_up():
        for group in range(groups):
            for fetch in fetches(group):
                fetch.start()
        squares[...] = jnp.zeros_like(squares)
        get_earlier.begin()
        entry = lax.broadcasted_iota(jnp.int32, (2 * SEGMENTS, LANES), 1)

        def spread(at, piece):
            square = jnp.broadcast_to(piece.astype(jnp.float32), (LANES, LANES))
            natural[pl.ds(at, LANES), :] = jnp.transpose(square)

        def mark(first, last):
            for step in range(first, last, 2):
                rows = [
                    natural[pl.ds(LANES + step + k, SEGMENTS, stride=steps), :] for k in range(2)
                ]
                found = jnp.concatenate(rows, axis=0)
                where = pl.ds((step + lead) * SEGMENTS, 2 * SEGMENTS)
                for at in range(0, vocab, LANES):
                    equal = found == (entry + at).astype(jnp.float32)
                    one_hot[where, at : at + LANES] = jnp.where(equal, 1.0, 0.0).astype(
                        jnp.bfloat16
                    )

        for at in range(0, tokens, LANES):
            spread(LANES + at, ids[:, at : at + LANES])
        mark(0, steps)
        get_earlier.finish()
        spread(0, earlier[:, tokens - LANES :])
        mark(-lead, 0)

    def project(raw):
        both = jnp.dot(
            one_hot[...],
            jnp.concatenate([tables[turn, s] for s in range(4)], axis=1),
            preferred_element_type=jnp.float32,
        )
        for s in range(4):
            for block in range(blocks):
                at = (s * blocks + block) * LANES
                raw[s, block] = both[:, at : at + LANES]

    def mix(block, raw):
        place = (turn - 1) * blocks + block
        here = lanes_of(place)
        feat_taps = [
            [wide_row(feat, (j, slice(s, s + 1), here)) for j in range(reach)] for s in range(3)
        ]
        inner_taps = [wide_row(inner, (slice(j, j + 1), here)) for j in range(span)]

        def row(s, step):
            return raw[s, block, pl.ds((step + lead) * SEGMENTS, SEGMENTS), :]

        mixed = []
        held = []
        pasts = [[], [], []]
        for step in range(-lead, steps):
            for s in range(3):
                if s == 0 and step < 1 - keep - reach:
                    continue
                pasts[s] = ([row(s + 1, step)] + pasts[s])[:reach]
            if step < reach - 1 - lead:
                continue
            keyed = weighted(feat_taps[1], pasts[1])
            valued = weighted(feat_taps[2], pasts[2])
            mixed = ([keyed * valued] + mixed)[:span]
            if step < -keep:
                continue
            queries = weighted(feat_taps[0], pasts[0])
            total = row(0, step) + queries * weighted(inner_taps, mixed)
            at = step + keep
            squares[pl.ds(at * SEGMENTS, SEGMENTS), :] += total * total
            held.append(total)
            if len(held) == 2:
                pair = jnp.concatenate(held, axis=0).astype(jnp.bfloat16)
                stream[place, pl.ds((at - 1) * SEGMENTS, 2 * SEGMENTS), :] = pair
                held = []

    raws = (raw_a, raw_b)

    def mix_all(raw):
        for block in range(blocks):
            mix(block, raw)

    def work(parity):
        for fetch in fetches(turn):
            fetch.wait()
        mix_all(raws[1 - parity])
        project(raws[parity])

    @pl.when(turn == 0)
    def _():
        set_up()
        for fetch in fetches(0):
            fetch.wait()
        project(raw_a)

    for parity in range(2):

        @pl.when((turn > 0) & (turn < groups) & (turn % 2 == parity))
        def _():
            work(parity)

    @pl.when(turn == groups)
    def _():
        mix_all(raws[(groups - 1) % 2])
        sums[...] = lax.dot_general(
            jnp.ones((SEGMENTS, LANES), jnp.float32),
            squares[...],
            (((1,), (1,)), ((), ())),
            precision=lax.Precision.HIGHEST,
            preferred_element_type=jnp.float32,
        )


def norm_step(peers, channels, sums, inverse, parts, send, recv):
    me = lax.axis_index("tp")

    def copy(slot, peer):
        return pltpu.make_async_remote_copy(
            src_ref=sums,
            dst_ref=parts.at[slot],
            send_sem=send.at[peer],
            recv_sem=recv.at[slot],
            device_id={"tp": peer},
            device_id_type=MESH,
        )

    others = [lax.rem(me + k, peers) for k in range(1, peers)]
    for peer in others:
        copy(me, peer).start()
    parts[me] = sums[...]
    for peer in others:
        copy(peer, peer).wait_recv()
    total = parts[0]
    for k in range(1, peers):
        total = total + parts[k]
    row = lax.rsqrt(total / channels + epsilon)
    for at in range(0, inverse.shape[0], LANES):
        block = jnp.broadcast_to(row[0:1, at : at + LANES], (LANES, LANES))
        inverse[pl.ds(at, LANES), :] = jnp.transpose(block)
    for peer in others:
        copy(me, peer).wait_send()


def local_part(
    keep, block, at_lanes, stream, inverse, feat, slope, weight, local, states, ends, product, powers
):
    steps = stream.shape[1] // SEGMENTS - keep
    modes = slope.shape[0]
    reach = feat.shape[0]
    place = lax.broadcasted_iota(jnp.int32, (SEGMENTS, LANES), 0)
    lanes = slice(at_lanes * LANES, (at_lanes + 1) * LANES)
    place_at = block * (ends.shape[2] // LANES) + at_lanes
    here = lanes_of(place_at)
    taps = [[wide_row(feat, (j, slice(s, s + 1), here)) for j in range(reach)] for s in (1, 2)]

    def normed_pair(at):
        where = pl.ds(pl.multiple_of(at * SEGMENTS, 2 * SEGMENTS), 2 * SEGMENTS)
        both = stream[place_at, where, :].astype(jnp.float32) * inverse[where, :]
        return both[:SEGMENTS], both[SEGMENTS:]

    past = ()
    for at in range(keep - even(reach - 1), keep, 2):
        past = tuple(reversed(normed_pair(at))) + past
    past = past[: reach - 1]

    def multiply(pair, past):
        products = []
        for value in normed_pair(keep + 2 * pair):
            series = (value,) + past
            products.append(weighted(taps[0], series) * weighted(taps[1], series))
            past = series[: reach - 1]
        where = pl.ds(pl.multiple_of(pair * 2 * SEGMENTS, 2 * SEGMENTS), 2 * SEGMENTS)
        rounded = jnp.concatenate(products, axis=0).astype(jnp.bfloat16)
        product[where, :] = rounded.astype(jnp.float32)
        return past

    lax.fori_loop(0, steps // 2, multiply, past, unroll=16)

    powers[0] = jnp.exp(-slope[:, here])
    leap = jnp.exp(slope[:, here] * float(-steps))
    for level in range(1, 4):
        powers[level] = leap
        leap = leap * leap
    rates = [wide_row(powers, (0, slice(m, m + 1))) for m in range(modes)]
    weights = [wide_row(weight, (slice(m, m + 1), here)) for m in range(modes)]

    def step(at, held):
        where = pl.ds(pl.multiple_of(at * SEGMENTS, SEGMENTS), SEGMENTS)
        value = product[where, :]
        held = tuple(rates[m] * held[m] + weights[m] * value for m in range(modes))
        local[block, at_lanes, where, :] = tree_sum(list(held))
        return held

    zero = jnp.zeros((SEGMENTS, LANES), jnp.float32)
    held = lax.fori_loop(0, steps, step, (zero,) * modes, unroll=16)
    for m in range(modes):
        leaps = [wide_row(powers, (1 + level, slice(m, m + 1))) for level in range(3)]
        total = jnp.where(place >= 1, pltpu.roll(held[m], 1, 0), 0.0)
        for level in range(3):
            reaching = 1 << level
            moved = leaps[level] * pltpu.roll(total, reaching, 0)
            total = total + jnp.where(place >= reaching, moved, 0.0)
        states[block, at_lanes, m] = total
        ended = leaps[0] * total + held[m]
        ends[block, m : m + 1, lanes] = ended[SEGMENTS - 1 :]


def whole_part(
    keep, block, at_lanes, stream, inverse, feat, slope, local, states, entering, out, powers, result
):
    steps = stream.shape[1] // SEGMENTS - keep
    modes = slope.shape[0]
    reach = feat.shape[0]
    place = lax.broadcasted_iota(jnp.int32, (SEGMENTS, LANES), 0)
    ahead = (place * -steps - 1).astype(jnp.float32)
    lanes = slice(at_lanes * LANES, (at_lanes + 1) * LANES)
    place_at = block * (entering.shape[2] // LANES) + at_lanes
    here = lanes_of(place_at)
    taps = [wide_row(feat, (j, slice(0, 1), here)) for j in range(reach)]
    powers[0] = jnp.exp(-slope[:, here])
    rates = [wide_row(powers, (0, slice(m, m + 1))) for m in range(modes)]

    def wide_pair(at):
        where = pl.ds(pl.multiple_of(at * SEGMENTS, 2 * SEGMENTS), 2 * SEGMENTS)
        both = stream[place_at, where, :].astype(jnp.float32)
        normed = both * inverse[where, :]
        halves = (slice(0, SEGMENTS), slice(SEGMENTS, 2 * SEGMENTS))
        return [(both[half], normed[half]) for half in halves]

    past = ()
    for at in range(keep - even(reach - 1), keep, 2):
        past = tuple(normed for _, normed in reversed(wide_pair(at))) + past
    past = past[: reach - 1]

    first = []
    for m in range(modes):
        reached = jnp.exp(wide_row(slope, (slice(m, m + 1), here)) * ahead)
        arriving = wide_row(entering, (block, slice(m, m + 1), lanes))
        first.append(rates[m] * states[block, at_lanes, m] + reached * arriving)

    def step(pair, carried):
        past, held = carried
        for half, (wide, normed) in enumerate(wide_pair(keep + 2 * pair)):
            at = 2 * pair + half
            series = (normed,) + past
            past = series[: reach - 1]
            where = pl.ds(pl.multiple_of(at * SEGMENTS, SEGMENTS), SEGMENTS)
            convolved = tree_sum(list(held)) + local[block, at_lanes, where, :]
            result[pl.ds(at, SEGMENTS, stride=steps), :] = wide + weighted(taps, series) * convolved
            held = tuple(rates[m] * held[m] for m in range(modes))
        return past, held

    lax.fori_loop(0, steps // 2, step, (past, tuple(first)), unroll=8)
    out[:, lanes] = result[...].astype(jnp.bfloat16)


class Halo:
    def __init__(self, begin, finish):
        self.begin = begin
        self.finish = finish


def kernel(
    lead,
    keep,
    count,
    peers,
    all_channels,
    ids,
    embed,
    proj,
    feat_one,
    inner,
    feat,
    slope,
    weight,
    out,
    stream,
    sums,
    raw_a,
    raw_b,
    squares,
    natural,
    one_hot,
    tables,
    earlier,
    inverse,
    parts,
    local,
    states,
    ends,
    arrived,
    carries,
    entering,
    product,
    powers,
    result,
    arrival,
    halo_sems,
    send_norm,
    recv_norm,
    send_out,
    recv_out,
    send_back,
    recv_back,
):
    now = pl.program_id(0)
    groups = tables.shape[0]
    turn = now - groups - 1
    me = lax.axis_index("ctx")
    owners, modes, width = ends.shape
    tokens = out.shape[0]
    blocks = width // LANES
    others = [lax.rem(me + k, count) for k in range(1, count)]

    halo = pltpu.make_async_remote_copy(
        src_ref=ids,
        dst_ref=earlier,
        send_sem=halo_sems.at[0],
        recv_sem=halo_sems.at[1],
        device_id={"ctx": lax.rem(me + 1, count)},
        device_id_type=MESH,
    )

    def begin():
        barrier = pltpu.get_barrier_semaphore()
        for peer in others:
            pl.semaphore_signal(barrier, inc=1, device_id={"ctx": peer}, device_id_type=MESH)
        mine = lax.axis_index("tp")
        for k in range(1, peers):
            peer = lax.rem(mine + k, peers)
            pl.semaphore_signal(barrier, inc=1, device_id={"tp": peer}, device_id_type=MESH)
        pl.semaphore_wait(barrier, count - 1 + peers - 1)

        @pl.when(me < count - 1)
        def _():
            halo.start()

    def finish():
        @pl.when(me > 0)
        def _():
            halo.wait_recv()

        @pl.when(me == 0)
        def _():
            earlier[...] = jnp.full_like(earlier, -1)

        @pl.when(me < count - 1)
        def _():
            halo.wait_send()

    first_part(
        now,
        lead,
        keep,
        Halo(begin, finish),
        earlier,
        ids,
        embed,
        proj,
        feat_one,
        inner,
        stream,
        sums,
        raw_a,
        raw_b,
        squares,
        natural,
        one_hot,
        tables,
        arrival,
    )

    @pl.when(now == groups)
    def _():
        norm_step(peers, all_channels, sums, inverse, parts, send_norm, recv_norm)

    def to_owner(slot, owner):
        return pltpu.make_async_remote_copy(
            src_ref=ends.at[owner],
            dst_ref=arrived.at[slot],
            send_sem=send_out.at[owner],
            recv_sem=recv_out.at[slot],
            device_id={"ctx": owner},
            device_id_type=MESH,
        )

    def from_owner(slot, peer):
        return pltpu.make_async_remote_copy(
            src_ref=carries.at[peer],
            dst_ref=entering.at[slot],
            send_sem=send_back.at[peer],
            recv_sem=recv_back.at[slot],
            device_id={"ctx": peer},
            device_id_type=MESH,
        )

    @pl.when((turn == me + owners // 2) & (me < owners))
    def _():
        lanes = pl.ds(pl.multiple_of(me * width, LANES), width)
        leap = jnp.exp(slope[:, lanes] * float(-tokens))
        arrived[me] = ends[me]
        for peer in others:
            to_owner(peer, me).wait_recv()
        carry = jnp.zeros((modes, width), jnp.float32)
        for source in range(count):
            carries[source] = carry
            carry = leap * carry + arrived[source]
        for peer in others:
            from_owner(me, peer).start()
        entering[me] = carries[me]

    @pl.when((turn >= 0) & (turn < owners))
    def _():
        for at in range(blocks):
            local_part(
                keep, turn, at, stream, inverse, feat, slope, weight, local, states, ends, product, powers
            )

        @pl.when(turn != me)
        def _():
            to_owner(me, turn).start()

    @pl.when(turn >= owners)
    def _():
        block = turn - owners

        @pl.when(block != me)
        def _():
            from_owner(block, me).wait_recv()

        for at in range(blocks):
            whole_part(
                keep, block, at, stream, inverse, feat, slope, local, states, entering, out, powers, result
            )

    @pl.when(turn == 2 * owners - 1)
    def _():
        for peer in others:

            @pl.when(peer < owners)
            def _():
                to_owner(me, peer).wait_send()

        @pl.when(me < owners)
        def _():
            for peer in others:
                from_owner(me, peer).wait_send()


def on_device(
    token_ids, embed_table, projected_table, feat_one, inner_taps, feat_two, decay, residue
):
    tokens = token_ids.shape[0]
    vocab, channels = embed_table.shape
    modes = decay.shape[1]
    count = lax.axis_size("ctx")
    peers = lax.axis_size("tp")
    steps = tokens // SEGMENTS
    keep = even(feat_two.shape[0] - 1)
    lead = even(keep + inner_taps.shape[0] - 1 + feat_one.shape[0] - 1)
    rows = (steps + keep) * SEGMENTS
    padded = -(-rows // LANES) * LANES
    proj = jnp.transpose(projected_table, (1, 0, 2))

    wide = min(256, channels)
    blocks = channels // wide
    extended = (steps + lead) * SEGMENTS
    size = max(LANES, channels // count)
    owners = channels // size
    begun = blocks + 1 + owners
    whole = lambda shape: pl.BlockSpec(shape, lambda c: (0,) * len(shape))
    raw = pltpu.VMEM((4, wide // LANES, extended, LANES), jnp.float32)
    shared = lambda number: pltpu.VMEM((number, modes, size), jnp.float32)
    return pl.pallas_call(
        functools.partial(kernel, lead, keep, count, peers, channels * peers),
        grid=(begun + owners,),
        in_specs=[
            whole((1, tokens)),
            pl.BlockSpec(memory_space=pl.ANY),
            pl.BlockSpec(memory_space=pl.ANY),
            whole(feat_one.shape),
            whole(inner_taps.shape),
            whole(feat_two.shape),
            whole((modes, channels)),
            whole((modes, channels)),
        ],
        out_specs=pl.BlockSpec((tokens, size), lambda c: (0, jnp.maximum(c - begun, 0))),
        out_shape=jax.ShapeDtypeStruct((tokens, channels), jnp.bfloat16),
        scratch_shapes=[
            pltpu.VMEM((channels // LANES, rows, LANES), jnp.bfloat16),
            pltpu.VMEM((SEGMENTS, padded), jnp.float32),
            raw,
            raw,
            pltpu.VMEM((padded, LANES), jnp.float32),
            pltpu.VMEM((LANES + tokens, LANES), jnp.float32),
            pltpu.VMEM((extended, vocab), jnp.bfloat16),
            pltpu.VMEM((blocks, 4, vocab, wide), jnp.bfloat16),
            pltpu.VMEM((1, tokens), jnp.int32),
            pltpu.VMEM((padded, LANES), jnp.float32),
            pltpu.VMEM((peers, SEGMENTS, padded), jnp.float32),
            pltpu.VMEM((owners, size // LANES, tokens, LANES), jnp.float32),
            pltpu.VMEM((owners, size // LANES, modes, SEGMENTS, LANES), jnp.float32),
            shared(owners),
            shared(count),
            shared(count),
            shared(owners),
            pltpu.VMEM((tokens, LANES), jnp.float32),
            pltpu.VMEM((4, modes, LANES), jnp.float32),
            pltpu.VMEM((tokens, LANES), jnp.float32),
            pltpu.SemaphoreType.DMA((blocks, 2)),
            pltpu.SemaphoreType.DMA((2,)),
            pltpu.SemaphoreType.DMA((peers,)),
            pltpu.SemaphoreType.DMA((peers,)),
        ]
        + [pltpu.SemaphoreType.DMA((count,))] * 4,
        compiler_params=pltpu.CompilerParams(
            dimension_semantics=("arbitrary",),
            collective_id=0,
            has_side_effects=True,
            vmem_limit_bytes=VMEM_LIMIT,
        ),
        name="hyena",
    )(
        token_ids[None],
        embed_table,
        proj,
        feat_one,
        inner_taps,
        feat_two,
        jnp.transpose(decay),
        jnp.transpose(residue),
    )


def solution(mesh):
    placed = (
        P("ctx"),
        P(None, "tp"),
        P(None, None, "tp"),
        P(None, None, "tp"),
        P(None, "tp"),
        P(None, None, "tp"),
        P("tp", None),
        P("tp", None),
    )
    return jax.shard_map(
        on_device, mesh=mesh, in_specs=placed, out_specs=P("ctx", "tp"), check_vma=False
    )
```

```python
import functools

import jax
import jax.numpy as jnp
from jax import lax
from jax.experimental import pallas as pl
from jax.experimental.pallas import tpu as pltpu
from jax.sharding import PartitionSpec as P

epsilon = 1e-06
HALO = 16
SEGMENTS = 8
LANES = 128
VMEM_LIMIT = 48 * 1024 * 1024
MESH = pl.DeviceIdType.MESH


def even(value):
    return value + value % 2


def wide_row(ref, index):
    return jnp.broadcast_to(ref[index], (SEGMENTS, LANES))


def lanes_of(block):
    return pl.ds(pl.multiple_of(block * LANES, LANES), LANES)


def weighted(taps, series):
    terms = [tap * value for tap, value in zip(taps, series)]
    total = terms[0]
    for term in terms[1:]:
        total = total + term
    return total


def tree_sum(terms):
    while len(terms) > 1:
        pairs = [a + b for a, b in zip(terms[::2], terms[1::2])]
        terms = pairs + terms[2 * len(pairs) :]
    return terms[0]


def first_part(
    turn,
    lead,
    keep,
    me,
    earlier,
    ids,
    embed,
    proj,
    feat,
    inner,
    stream,
    sums,
    raw_a,
    raw_b,
    squares,
    natural,
    one_hot,
    tables,
    arrival,
):
    groups, _, vocab, width = tables.shape
    blocks = width // LANES
    tokens = ids.shape[1]
    steps = tokens // SEGMENTS
    reach = feat.shape[0]
    span = inner.shape[0]

    def fetches(group):
        lanes = pl.ds(pl.multiple_of(group * width, LANES), width)
        return (
            pltpu.make_async_copy(
                embed.at[:, lanes], tables.at[group, 0], arrival.at[group, 0]
            ),
            pltpu.make_async_copy(
                proj.at[:, :, lanes], tables.at[group, pl.ds(1, 3)], arrival.at[group, 1]
            ),
        )

    def set_up():
        for group in range(groups):
            for fetch in fetches(group):
                fetch.start()
        squares[...] = jnp.zeros_like(squares)
        entry = lax.broadcasted_iota(jnp.int32, (2 * SEGMENTS, LANES), 1)

        def spread(at, piece):
            square = jnp.broadcast_to(piece.astype(jnp.float32), (LANES, LANES))
            natural[pl.ds(at, LANES), :] = jnp.transpose(square)

        def mark(first, last):
            for step in range(first, last, 2):
                rows = [
                    natural[pl.ds(LANES + step + k, SEGMENTS, stride=steps), :] for k in range(2)
                ]
                found = jnp.concatenate(rows, axis=0)
                where = pl.ds((step + lead) * SEGMENTS, 2 * SEGMENTS)
                for at in range(0, vocab, LANES):
                    equal = found == (entry + at).astype(jnp.float32)
                    one_hot[where, at : at + LANES] = jnp.where(equal, 1.0, 0.0).astype(
                        jnp.bfloat16
                    )

        for at in range(0, tokens, LANES):
            spread(LANES + at, ids[:, at : at + LANES])
        spread(0, jnp.where(me == 0, -1, earlier[:, tokens - LANES :]))
        mark(-lead, steps)

    def project(raw):
        both = jnp.dot(
            one_hot[...],
            jnp.concatenate([tables[turn, s] for s in range(4)], axis=1),
            preferred_element_type=jnp.float32,
        )
        for s in range(4):
            for block in range(blocks):
                at = (s * blocks + block) * LANES
                raw[s, block] = both[:, at : at + LANES]

    def mix(block, raw):
        place = (turn - 1) * blocks + block
        here = lanes_of(place)
        feat_taps = [
            [wide_row(feat, (j, slice(s, s + 1), here)) for j in range(reach)] for s in range(3)
        ]
        inner_taps = [wide_row(inner, (slice(j, j + 1), here)) for j in range(span)]

        def row(s, step):
            return raw[s, block, pl.ds((step + lead) * SEGMENTS, SEGMENTS), :]

        mixed = []
        held = []
        pasts = [[], [], []]
        for step in range(-lead, steps):
            for s in range(3):
                if s == 0 and step < 1 - keep - reach:
                    continue
                pasts[s] = ([row(s + 1, step)] + pasts[s])[:reach]
            if step < reach - 1 - lead:
                continue
            keyed = weighted(feat_taps[1], pasts[1])
            valued = weighted(feat_taps[2], pasts[2])
            mixed = ([keyed * valued] + mixed)[:span]
            if step < -keep:
                continue
            queries = weighted(feat_taps[0], pasts[0])
            total = row(0, step) + queries * weighted(inner_taps, mixed)
            at = step + keep
            squares[pl.ds(at * SEGMENTS, SEGMENTS), :] += total * total
            held.append(total)
            if len(held) == 2:
                pair = jnp.concatenate(held, axis=0).astype(jnp.bfloat16)
                stream[place, pl.ds((at - 1) * SEGMENTS, 2 * SEGMENTS), :] = pair
                held = []

    raws = (raw_a, raw_b)

    def mix_all(raw):
        for block in range(blocks):
            mix(block, raw)

    def work(parity):
        for fetch in fetches(turn):
            fetch.wait()
        mix_all(raws[1 - parity])
        project(raws[parity])

    @pl.when(turn == 0)
    def _():
        set_up()
        for fetch in fetches(0):
            fetch.wait()
        project(raw_a)

    for parity in range(2):

        @pl.when((turn > 0) & (turn < groups) & (turn % 2 == parity))
        def _():
            work(parity)

    @pl.when(turn == groups)
    def _():
        mix_all(raws[(groups - 1) % 2])
        sums[...] = lax.dot_general(
            jnp.ones((SEGMENTS, LANES), jnp.float32),
            squares[...],
            (((1,), (1,)), ((), ())),
            precision=lax.Precision.HIGHEST,
            preferred_element_type=jnp.float32,
        )


def norm_step(peers, channels, sums, inverse, parts, send, recv):
    me = lax.axis_index("tp")

    def copy(slot, peer):
        return pltpu.make_async_remote_copy(
            src_ref=sums,
            dst_ref=parts.at[slot],
            send_sem=send.at[peer],
            recv_sem=recv.at[slot],
            device_id={"tp": peer},
            device_id_type=MESH,
        )

    others = [lax.rem(me + k, peers) for k in range(1, peers)]
    for peer in others:
        copy(me, peer).start()
    parts[me] = sums[...]
    for peer in others:
        copy(peer, peer).wait_recv()
    total = parts[0]
    for k in range(1, peers):
        total = total + parts[k]
    row = lax.rsqrt(total / channels + epsilon)
    for at in range(0, inverse.shape[0], LANES):
        block = jnp.broadcast_to(row[0:1, at : at + LANES], (LANES, LANES))
        inverse[pl.ds(at, LANES), :] = jnp.transpose(block)
    for peer in others:
        copy(me, peer).wait_send()


def local_part(
    keep, block, at_lanes, stream, inverse, feat, slope, weight, local, states, ends, product, powers
):
    steps = stream.shape[1] // SEGMENTS - keep
    modes = slope.shape[0]
    reach = feat.shape[0]
    place = lax.broadcasted_iota(jnp.int32, (SEGMENTS, LANES), 0)
    lanes = slice(at_lanes * LANES, (at_lanes + 1) * LANES)
    place_at = block * (ends.shape[2] // LANES) + at_lanes
    here = lanes_of(place_at)
    taps = [[wide_row(feat, (j, slice(s, s + 1), here)) for j in range(reach)] for s in (1, 2)]

    def normed_pair(at):
        where = pl.ds(pl.multiple_of(at * SEGMENTS, 2 * SEGMENTS), 2 * SEGMENTS)
        both = stream[place_at, where, :].astype(jnp.float32) * inverse[where, :]
        return both[:SEGMENTS], both[SEGMENTS:]

    past = ()
    for at in range(keep - even(reach - 1), keep, 2):
        past = tuple(reversed(normed_pair(at))) + past
    past = past[: reach - 1]

    def multiply(pair, past):
        products = []
        for value in normed_pair(keep + 2 * pair):
            series = (value,) + past
            products.append(weighted(taps[0], series) * weighted(taps[1], series))
            past = series[: reach - 1]
        where = pl.ds(pl.multiple_of(pair * 2 * SEGMENTS, 2 * SEGMENTS), 2 * SEGMENTS)
        rounded = jnp.concatenate(products, axis=0).astype(jnp.bfloat16)
        product[where, :] = rounded.astype(jnp.float32)
        return past

    lax.fori_loop(0, steps // 2, multiply, past, unroll=16)

    powers[0] = jnp.exp(-slope[:, here])
    leap = jnp.exp(slope[:, here] * float(-steps))
    for level in range(1, 4):
        powers[level] = leap
        leap = leap * leap
    rates = [wide_row(powers, (0, slice(m, m + 1))) for m in range(modes)]
    weights = [wide_row(weight, (slice(m, m + 1), here)) for m in range(modes)]

    def step(at, held):
        where = pl.ds(pl.multiple_of(at * SEGMENTS, SEGMENTS), SEGMENTS)
        value = product[where, :]
        held = tuple(rates[m] * held[m] + weights[m] * value for m in range(modes))
        local[block, at_lanes, where, :] = tree_sum(list(held))
        return held

    zero = jnp.zeros((SEGMENTS, LANES), jnp.float32)
    held = lax.fori_loop(0, steps, step, (zero,) * modes, unroll=16)
    for m in range(modes):
        leaps = [wide_row(powers, (1 + level, slice(m, m + 1))) for level in range(3)]
        total = jnp.where(place >= 1, pltpu.roll(held[m], 1, 0), 0.0)
        for level in range(3):
            reaching = 1 << level
            moved = leaps[level] * pltpu.roll(total, reaching, 0)
            total = total + jnp.where(place >= reaching, moved, 0.0)
        states[block, at_lanes, m] = total
        ended = leaps[0] * total + held[m]
        ends[block, m : m + 1, lanes] = ended[SEGMENTS - 1 :]


def whole_part(
    keep, block, at_lanes, stream, inverse, feat, slope, local, states, entering, out, powers, result
):
    steps = stream.shape[1] // SEGMENTS - keep
    modes = slope.shape[0]
    reach = feat.shape[0]
    place = lax.broadcasted_iota(jnp.int32, (SEGMENTS, LANES), 0)
    ahead = (place * -steps - 1).astype(jnp.float32)
    lanes = slice(at_lanes * LANES, (at_lanes + 1) * LANES)
    place_at = block * (entering.shape[2] // LANES) + at_lanes
    here = lanes_of(place_at)
    taps = [wide_row(feat, (j, slice(0, 1), here)) for j in range(reach)]
    powers[0] = jnp.exp(-slope[:, here])
    rates = [wide_row(powers, (0, slice(m, m + 1))) for m in range(modes)]

    def wide_pair(at):
        where = pl.ds(pl.multiple_of(at * SEGMENTS, 2 * SEGMENTS), 2 * SEGMENTS)
        both = stream[place_at, where, :].astype(jnp.float32)
        normed = both * inverse[where, :]
        halves = (slice(0, SEGMENTS), slice(SEGMENTS, 2 * SEGMENTS))
        return [(both[half], normed[half]) for half in halves]

    past = ()
    for at in range(keep - even(reach - 1), keep, 2):
        past = tuple(normed for _, normed in reversed(wide_pair(at))) + past
    past = past[: reach - 1]

    first = []
    for m in range(modes):
        reached = jnp.exp(wide_row(slope, (slice(m, m + 1), here)) * ahead)
        arriving = wide_row(entering, (block, slice(m, m + 1), lanes))
        first.append(rates[m] * states[block, at_lanes, m] + reached * arriving)

    def step(pair, carried):
        past, held = carried
        for half, (wide, normed) in enumerate(wide_pair(keep + 2 * pair)):
            at = 2 * pair + half
            series = (normed,) + past
            past = series[: reach - 1]
            where = pl.ds(pl.multiple_of(at * SEGMENTS, SEGMENTS), SEGMENTS)
            convolved = tree_sum(list(held)) + local[block, at_lanes, where, :]
            result[pl.ds(at, SEGMENTS, stride=steps), :] = wide + weighted(taps, series) * convolved
            held = tuple(rates[m] * held[m] for m in range(modes))
        return past, held

    lax.fori_loop(0, steps // 2, step, (past, tuple(first)), unroll=8)
    out[:, lanes] = result[...].astype(jnp.bfloat16)


def kernel(
    lead,
    keep,
    count,
    peers,
    all_channels,
    earlier,
    ids,
    embed,
    proj,
    feats,
    inner,
    rates,
    out,
    stream,
    sums,
    raw_a,
    raw_b,
    squares,
    natural,
    one_hot,
    tables,
    inverse,
    parts,
    local,
    states,
    ends,
    arrived,
    carries,
    entering,
    product,
    powers,
    result,
    arrival,
    send_norm,
    recv_norm,
    send_out,
    recv_out,
    send_back,
    recv_back,
):
    reach = feats.shape[0] // 2
    feat_one, feat = feats.at[pl.ds(0, reach)], feats.at[pl.ds(reach, reach)]
    modes = rates.shape[0] // 2
    slope, weight = rates.at[pl.ds(0, modes)], rates.at[pl.ds(modes, modes)]
    now = pl.program_id(0)
    groups = tables.shape[0]
    turn = now - groups - 1
    me = lax.axis_index("ctx")
    owners, modes, width = ends.shape
    tokens = out.shape[0]
    blocks = width // LANES
    others = [lax.rem(me + k, count) for k in range(1, count)]

    barrier = pltpu.get_barrier_semaphore()

    @pl.when(now == 0)
    def _():
        for peer in others:
            pl.semaphore_signal(barrier, inc=1, device_id={"ctx": peer}, device_id_type=MESH)
        mine = lax.axis_index("tp")
        for k in range(1, peers):
            peer = lax.rem(mine + k, peers)
            pl.semaphore_signal(barrier, inc=1, device_id={"tp": peer}, device_id_type=MESH)

    first_part(
        now,
        lead,
        keep,
        me,
        earlier,
        ids,
        embed,
        proj,
        feat_one,
        inner,
        stream,
        sums,
        raw_a,
        raw_b,
        squares,
        natural,
        one_hot,
        tables,
        arrival,
    )

    @pl.when(now == groups)
    def _():
        pl.semaphore_wait(barrier, count - 1 + peers - 1)
        norm_step(peers, all_channels, sums, inverse, parts, send_norm, recv_norm)

    def to_owner(slot, owner):
        return pltpu.make_async_remote_copy(
            src_ref=ends.at[owner],
            dst_ref=arrived.at[slot],
            send_sem=send_out.at[owner],
            recv_sem=recv_out.at[slot],
            device_id={"ctx": owner},
            device_id_type=MESH,
        )

    def from_owner(slot, peer):
        return pltpu.make_async_remote_copy(
            src_ref=carries.at[peer],
            dst_ref=entering.at[slot],
            send_sem=send_back.at[peer],
            recv_sem=recv_back.at[slot],
            device_id={"ctx": peer},
            device_id_type=MESH,
        )

    @pl.when((turn == me + owners // 2) & (me < owners))
    def _():
        lanes = pl.ds(pl.multiple_of(me * width, LANES), width)
        leap = jnp.exp(slope[:, lanes] * float(-tokens))
        arrived[me] = ends[me]
        for peer in others:
            to_owner(peer, me).wait_recv()
        carry = jnp.zeros((modes, width), jnp.float32)
        for source in range(count):
            carries[source] = carry
            carry = leap * carry + arrived[source]
        for peer in others:
            from_owner(me, peer).start()
        entering[me] = carries[me]

    @pl.when((turn >= 0) & (turn < owners))
    def _():
        for at in range(blocks):
            local_part(
                keep, turn, at, stream, inverse, feat, slope, weight, local, states, ends, product, powers
            )

        @pl.when(turn != me)
        def _():
            to_owner(me, turn).start()

    @pl.when(turn >= owners)
    def _():
        block = turn - owners

        @pl.when(block != me)
        def _():
            from_owner(block, me).wait_recv()

        for at in range(blocks):
            whole_part(
                keep, block, at, stream, inverse, feat, slope, local, states, entering, out, powers, result
            )

    @pl.when(turn == 2 * owners - 1)
    def _():
        for peer in others:

            @pl.when(peer < owners)
            def _():
                to_owner(me, peer).wait_send()

        @pl.when(me < owners)
        def _():
            for peer in others:
                from_owner(me, peer).wait_send()


def on_device(
    token_ids, embed_table, projected_table, feat_one, inner_taps, feat_two, decay, residue
):
    tokens = token_ids.shape[0]
    vocab, channels = embed_table.shape
    modes = decay.shape[1]
    count = lax.axis_size("ctx")
    peers = lax.axis_size("tp")
    steps = tokens // SEGMENTS
    keep = even(feat_two.shape[0] - 1)
    lead = even(keep + inner_taps.shape[0] - 1 + feat_one.shape[0] - 1)
    rows = (steps + keep) * SEGMENTS
    padded = -(-rows // LANES) * LANES
    earlier = lax.ppermute(token_ids, "ctx", [(source, source + 1) for source in range(count - 1)])
    feats = jnp.concatenate([feat_one, feat_two])
    rates = jnp.concatenate([jnp.transpose(decay), jnp.transpose(residue)])
    proj = jnp.transpose(projected_table, (1, 0, 2))

    wide = min(256, channels)
    blocks = channels // wide
    extended = (steps + lead) * SEGMENTS
    size = max(LANES, channels // count)
    owners = channels // size
    begun = blocks + 1 + owners
    whole = lambda shape: pl.BlockSpec(shape, lambda c: (0,) * len(shape))
    raw = pltpu.VMEM((4, wide // LANES, extended, LANES), jnp.float32)
    shared = lambda number: pltpu.VMEM((number, modes, size), jnp.float32)
    return pl.pallas_call(
        functools.partial(kernel, lead, keep, count, peers, channels * peers),
        grid=(begun + owners,),
        in_specs=[
            whole((1, tokens)),
            whole((1, tokens)),
            pl.BlockSpec(memory_space=pl.ANY),
            pl.BlockSpec(memory_space=pl.ANY),
            whole(feats.shape),
            whole(inner_taps.shape),
            whole(rates.shape),
        ],
        out_specs=pl.BlockSpec((tokens, size), lambda c: (0, jnp.maximum(c - begun, 0))),
        out_shape=jax.ShapeDtypeStruct((tokens, channels), jnp.bfloat16),
        scratch_shapes=[
            pltpu.VMEM((channels // LANES, rows, LANES), jnp.bfloat16),
            pltpu.VMEM((SEGMENTS, padded), jnp.float32),
            raw,
            raw,
            pltpu.VMEM((padded, LANES), jnp.float32),
            pltpu.VMEM((LANES + tokens, LANES), jnp.float32),
            pltpu.VMEM((extended, vocab), jnp.bfloat16),
            pltpu.VMEM((blocks, 4, vocab, wide), jnp.bfloat16),
            pltpu.VMEM((padded, LANES), jnp.float32),
            pltpu.VMEM((peers, SEGMENTS, padded), jnp.float32),
            pltpu.VMEM((owners, size // LANES, tokens, LANES), jnp.float32),
            pltpu.VMEM((owners, size // LANES, modes, SEGMENTS, LANES), jnp.float32),
            shared(owners),
            shared(count),
            shared(count),
            shared(owners),
            pltpu.VMEM((tokens, LANES), jnp.float32),
            pltpu.VMEM((4, modes, LANES), jnp.float32),
            pltpu.VMEM((tokens, LANES), jnp.float32),
            pltpu.SemaphoreType.DMA((blocks, 2)),
            pltpu.SemaphoreType.DMA((peers,)),
            pltpu.SemaphoreType.DMA((peers,)),
        ]
        + [pltpu.SemaphoreType.DMA((count,))] * 4,
        compiler_params=pltpu.CompilerParams(
            dimension_semantics=("arbitrary",),
            collective_id=0,
            has_side_effects=True,
            vmem_limit_bytes=VMEM_LIMIT,
        ),
        name="hyena",
    )(
        earlier[None],
        token_ids[None],
        embed_table,
        proj,
        feats,
        inner_taps,
        rates,
    )


def solution(mesh):
    placed = (
        P("ctx"),
        P(None, "tp"),
        P(None, None, "tp"),
        P(None, None, "tp"),
        P(None, "tp"),
        P(None, None, "tp"),
        P("tp", None),
        P("tp", None),
    )
    return jax.shard_map(
        on_device, mesh=mesh, in_specs=placed, out_specs=P("ctx", "tp"), check_vma=False
    )
```

```python
import functools

import jax
import jax.numpy as jnp
from jax import lax
from jax.experimental import pallas as pl
from jax.experimental.pallas import tpu as pltpu
from jax.sharding import PartitionSpec as P

epsilon = 1e-06
HALO = 16
SEGMENTS = 8
LANES = 128
VMEM_LIMIT = 48 * 1024 * 1024
MESH = pl.DeviceIdType.MESH


def even(value):
    return value + value % 2


def wide_row(ref, index):
    return jnp.broadcast_to(ref[index], (SEGMENTS, LANES))


def lanes_of(block):
    return pl.ds(pl.multiple_of(block * LANES, LANES), LANES)


def weighted(taps, series):
    terms = [tap * value for tap, value in zip(taps, series)]
    total = terms[0]
    for term in terms[1:]:
        total = total + term
    return total


def tree_sum(terms):
    while len(terms) > 1:
        pairs = [a + b for a, b in zip(terms[::2], terms[1::2])]
        terms = pairs + terms[2 * len(pairs) :]
    return terms[0]


def first_part(
    turn,
    lead,
    keep,
    me,
    earlier,
    ids,
    embed,
    proj,
    feat,
    inner,
    stream,
    sums,
    raw_a,
    raw_b,
    squares,
    natural,
    one_hot,
    tables,
    arrival,
):
    groups, _, vocab, width = tables.shape
    blocks = width // LANES
    tokens = ids.shape[1]
    steps = tokens // SEGMENTS
    reach = feat.shape[0]
    span = inner.shape[0]

    def fetches(group):
        lanes = pl.ds(pl.multiple_of(group * width, LANES), width)
        return (
            pltpu.make_async_copy(
                embed.at[:, lanes], tables.at[group, 0], arrival.at[group, 0]
            ),
            pltpu.make_async_copy(
                proj.at[:, :, lanes], tables.at[group, pl.ds(1, 3)], arrival.at[group, 1]
            ),
        )

    def set_up():
        for group in range(groups):
            for fetch in fetches(group):
                fetch.start()
        squares[...] = jnp.zeros_like(squares)
        entry = lax.broadcasted_iota(jnp.int32, (2 * SEGMENTS, LANES), 1)

        def spread(at, piece):
            square = jnp.broadcast_to(piece.astype(jnp.float32), (LANES, LANES))
            natural[pl.ds(at, LANES), :] = jnp.transpose(square)

        def mark(first, last):
            for step in range(first, last, 2):
                rows = [
                    natural[pl.ds(LANES + step + k, SEGMENTS, stride=steps), :] for k in range(2)
                ]
                found = jnp.concatenate(rows, axis=0)
                where = pl.ds((step + lead) * SEGMENTS, 2 * SEGMENTS)
                for at in range(0, vocab, LANES):
                    equal = found == (entry + at).astype(jnp.float32)
                    one_hot[where, at : at + LANES] = jnp.where(equal, 1.0, 0.0).astype(
                        jnp.bfloat16
                    )

        for at in range(0, tokens, LANES):
            spread(LANES + at, ids[:, at : at + LANES])
        spread(0, jnp.where(me == 0, -1, earlier[:, tokens - LANES :]))
        mark(-lead, steps)

    def project(raw):
        both = jnp.dot(
            one_hot[...],
            jnp.concatenate([tables[turn, s] for s in range(4)], axis=1),
            preferred_element_type=jnp.float32,
        )
        for s in range(4):
            for block in range(blocks):
                at = (s * blocks + block) * LANES
                raw[s, block] = both[:, at : at + LANES]

    def mix(block, raw):
        place = (turn - 1) * blocks + block
        here = lanes_of(place)
        feat_taps = [
            [wide_row(feat, (j, slice(s, s + 1), here)) for j in range(reach)] for s in range(3)
        ]
        inner_taps = [wide_row(inner, (slice(j, j + 1), here)) for j in range(span)]

        def row(s, step):
            return raw[s, block, pl.ds((step + lead) * SEGMENTS, SEGMENTS), :]

        mixed = []
        held = []
        pasts = [[], [], []]
        for step in range(-lead, steps):
            for s in range(3):
                if s == 0 and step < 1 - keep - reach:
                    continue
                pasts[s] = ([row(s + 1, step)] + pasts[s])[:reach]
            if step < reach - 1 - lead:
                continue
            keyed = weighted(feat_taps[1], pasts[1])
            valued = weighted(feat_taps[2], pasts[2])
            mixed = ([keyed * valued] + mixed)[:span]
            if step < -keep:
                continue
            queries = weighted(feat_taps[0], pasts[0])
            total = row(0, step) + queries * weighted(inner_taps, mixed)
            at = step + keep
            squares[pl.ds(at * SEGMENTS, SEGMENTS), :] += total * total
            held.append(total)
            if len(held) == 2:
                pair = jnp.concatenate(held, axis=0).astype(jnp.bfloat16)
                stream[place, pl.ds((at - 1) * SEGMENTS, 2 * SEGMENTS), :] = pair
                held = []

    raws = (raw_a, raw_b)

    def mix_all(raw):
        for block in range(blocks):
            mix(block, raw)

    def work(parity):
        for fetch in fetches(turn):
            fetch.wait()
        mix_all(raws[1 - parity])
        project(raws[parity])

    @pl.when(turn == 0)
    def _():
        set_up()
        for fetch in fetches(0):
            fetch.wait()
        project(raw_a)

    for parity in range(2):

        @pl.when((turn > 0) & (turn < groups) & (turn % 2 == parity))
        def _():
            work(parity)

    @pl.when(turn == groups)
    def _():
        mix_all(raws[(groups - 1) % 2])
        sums[...] = lax.dot_general(
            jnp.ones((SEGMENTS, LANES), jnp.float32),
            squares[...],
            (((1,), (1,)), ((), ())),
            precision=lax.Precision.HIGHEST,
            preferred_element_type=jnp.float32,
        )


def norm_step(peers, channels, sums, inverse, parts, send, recv):
    me = lax.axis_index("tp")

    def copy(slot, peer):
        return pltpu.make_async_remote_copy(
            src_ref=sums,
            dst_ref=parts.at[slot],
            send_sem=send.at[peer],
            recv_sem=recv.at[slot],
            device_id={"tp": peer},
            device_id_type=MESH,
        )

    others = [lax.rem(me + k, peers) for k in range(1, peers)]
    for peer in others:
        copy(me, peer).start()
    parts[me] = sums[...]
    for peer in others:
        copy(peer, peer).wait_recv()
    total = parts[0]
    for k in range(1, peers):
        total = total + parts[k]
    row = lax.rsqrt(total / channels + epsilon)
    for at in range(0, inverse.shape[0], LANES):
        block = jnp.broadcast_to(row[0:1, at : at + LANES], (LANES, LANES))
        inverse[pl.ds(at, LANES), :] = jnp.transpose(block)
    for peer in others:
        copy(me, peer).wait_send()


def local_part(
    keep, block, at_lanes, stream, inverse, feat, slope, weight, local, states, ends, product, powers
):
    steps = stream.shape[1] // SEGMENTS - keep
    modes = slope.shape[0]
    reach = feat.shape[0]
    place = lax.broadcasted_iota(jnp.int32, (SEGMENTS, LANES), 0)
    lanes = slice(at_lanes * LANES, (at_lanes + 1) * LANES)
    place_at = block * (ends.shape[2] // LANES) + at_lanes
    here = lanes_of(place_at)
    taps = [[wide_row(feat, (j, slice(s, s + 1), here)) for j in range(reach)] for s in (1, 2)]

    def normed_pair(at):
        where = pl.ds(pl.multiple_of(at * SEGMENTS, 2 * SEGMENTS), 2 * SEGMENTS)
        both = stream[place_at, where, :].astype(jnp.float32) * inverse[where, :]
        return both[:SEGMENTS], both[SEGMENTS:]

    past = ()
    for at in range(keep - even(reach - 1), keep, 2):
        past = tuple(reversed(normed_pair(at))) + past
    past = past[: reach - 1]

    def multiply(pair, past):
        products = []
        for value in normed_pair(keep + 2 * pair):
            series = (value,) + past
            products.append(weighted(taps[0], series) * weighted(taps[1], series))
            past = series[: reach - 1]
        where = pl.ds(pl.multiple_of(pair * 2 * SEGMENTS, 2 * SEGMENTS), 2 * SEGMENTS)
        rounded = jnp.concatenate(products, axis=0).astype(jnp.bfloat16)
        product[where, :] = rounded.astype(jnp.float32)
        return past

    lax.fori_loop(0, steps // 2, multiply, past, unroll=16)

    powers[0] = jnp.exp(-slope[:, here])
    leap = jnp.exp(slope[:, here] * float(-steps))
    for level in range(1, 4):
        powers[level] = leap
        leap = leap * leap
    rates = [wide_row(powers, (0, slice(m, m + 1))) for m in range(modes)]
    weights = [wide_row(weight, (slice(m, m + 1), here)) for m in range(modes)]

    def step(at, held):
        where = pl.ds(pl.multiple_of(at * SEGMENTS, SEGMENTS), SEGMENTS)
        value = product[where, :]
        held = tuple(rates[m] * held[m] + weights[m] * value for m in range(modes))
        local[block, at_lanes, where, :] = tree_sum(list(held))
        return held

    zero = jnp.zeros((SEGMENTS, LANES), jnp.float32)
    held = lax.fori_loop(0, steps, step, (zero,) * modes, unroll=16)
    for m in range(modes):
        leaps = [wide_row(powers, (1 + level, slice(m, m + 1))) for level in range(3)]
        total = jnp.where(place >= 1, pltpu.roll(held[m], 1, 0), 0.0)
        for level in range(3):
            reaching = 1 << level
            moved = leaps[level] * pltpu.roll(total, reaching, 0)
            total = total + jnp.where(place >= reaching, moved, 0.0)
        states[block, at_lanes, m] = total
        ended = leaps[0] * total + held[m]
        ends[block, m : m + 1, lanes] = ended[SEGMENTS - 1 :]


def whole_part(
    keep, block, at_lanes, stream, inverse, feat, slope, local, states, entering, out, powers, result
):
    steps = stream.shape[1] // SEGMENTS - keep
    modes = slope.shape[0]
    reach = feat.shape[0]
    place = lax.broadcasted_iota(jnp.int32, (SEGMENTS, LANES), 0)
    ahead = (place * -steps - 1).astype(jnp.float32)
    lanes = slice(at_lanes * LANES, (at_lanes + 1) * LANES)
    place_at = block * (entering.shape[2] // LANES) + at_lanes
    here = lanes_of(place_at)
    taps = [wide_row(feat, (j, slice(0, 1), here)) for j in range(reach)]
    powers[0] = jnp.exp(-slope[:, here])
    rates = [wide_row(powers, (0, slice(m, m + 1))) for m in range(modes)]

    def wide_pair(at):
        where = pl.ds(pl.multiple_of(at * SEGMENTS, 2 * SEGMENTS), 2 * SEGMENTS)
        both = stream[place_at, where, :].astype(jnp.float32)
        normed = both * inverse[where, :]
        halves = (slice(0, SEGMENTS), slice(SEGMENTS, 2 * SEGMENTS))
        return [(both[half], normed[half]) for half in halves]

    past = ()
    for at in range(keep - even(reach - 1), keep, 2):
        past = tuple(normed for _, normed in reversed(wide_pair(at))) + past
    past = past[: reach - 1]

    first = []
    for m in range(modes):
        reached = jnp.exp(wide_row(slope, (slice(m, m + 1), here)) * ahead)
        arriving = wide_row(entering, (block, slice(m, m + 1), lanes))
        first.append(rates[m] * states[block, at_lanes, m] + reached * arriving)

    def step(pair, carried):
        past, held = carried
        for half, (wide, normed) in enumerate(wide_pair(keep + 2 * pair)):
            at = 2 * pair + half
            series = (normed,) + past
            past = series[: reach - 1]
            where = pl.ds(pl.multiple_of(at * SEGMENTS, SEGMENTS), SEGMENTS)
            convolved = tree_sum(list(held)) + local[block, at_lanes, where, :]
            result[pl.ds(at, SEGMENTS, stride=steps), :] = wide + weighted(taps, series) * convolved
            held = tuple(rates[m] * held[m] for m in range(modes))
        return past, held

    lax.fori_loop(0, steps // 2, step, (past, tuple(first)), unroll=8)
    out[:, lanes] = result[...].astype(jnp.bfloat16)


def kernel(
    lead,
    keep,
    count,
    peers,
    all_channels,
    earlier,
    ids,
    embed,
    proj,
    feats,
    inner,
    rates,
    out,
    stream,
    sums,
    raw_a,
    raw_b,
    squares,
    natural,
    one_hot,
    tables,
    inverse,
    parts,
    local,
    states,
    ends,
    arrived,
    carries,
    entering,
    product,
    powers,
    result,
    arrival,
    send_norm,
    recv_norm,
    send_out,
    recv_out,
    send_back,
    recv_back,
):
    reach = feats.shape[0] // 2
    feat_one, feat = feats.at[pl.ds(0, reach)], feats.at[pl.ds(reach, reach)]
    modes = rates.shape[0] // 2
    slope, weight = rates.at[pl.ds(0, modes)], rates.at[pl.ds(modes, modes)]
    now = pl.program_id(0)
    groups = tables.shape[0]
    turn = now - groups - 1
    me = lax.axis_index("ctx")
    owners, modes, width = ends.shape
    tokens = out.shape[0]
    blocks = width // LANES
    others = [lax.rem(me + k, count) for k in range(1, count)]

    barrier = pltpu.get_barrier_semaphore()

    @pl.when(now == 0)
    def _():
        for peer in others:
            pl.semaphore_signal(barrier, inc=1, device_id={"ctx": peer}, device_id_type=MESH)
        mine = lax.axis_index("tp")
        for k in range(1, peers):
            peer = lax.rem(mine + k, peers)
            pl.semaphore_signal(barrier, inc=1, device_id={"tp": peer}, device_id_type=MESH)

    first_part(
        now,
        lead,
        keep,
        me,
        earlier,
        ids,
        embed,
        proj,
        feat_one,
        inner,
        stream,
        sums,
        raw_a,
        raw_b,
        squares,
        natural,
        one_hot,
        tables,
        arrival,
    )

    @pl.when(now == groups)
    def _():
        pl.semaphore_wait(barrier, count - 1 + peers - 1)
        norm_step(peers, all_channels, sums, inverse, parts, send_norm, recv_norm)

    def to_owner(slot, owner):
        return pltpu.make_async_remote_copy(
            src_ref=ends.at[owner],
            dst_ref=arrived.at[slot],
            send_sem=send_out.at[owner],
            recv_sem=recv_out.at[slot],
            device_id={"ctx": owner},
            device_id_type=MESH,
        )

    def from_owner(slot, peer):
        return pltpu.make_async_remote_copy(
            src_ref=carries.at[peer],
            dst_ref=entering.at[slot],
            send_sem=send_back.at[peer],
            recv_sem=recv_back.at[slot],
            device_id={"ctx": peer},
            device_id_type=MESH,
        )

    @pl.when((turn == me + owners // 2) & (me < owners))
    def _():
        lanes = pl.ds(pl.multiple_of(me * width, LANES), width)
        leap = jnp.exp(slope[:, lanes] * float(-tokens))
        arrived[me] = ends[me]
        for peer in others:
            to_owner(peer, me).wait_recv()
        carry = jnp.zeros((modes, width), jnp.float32)
        for source in range(count):
            carries[source] = carry
            carry = leap * carry + arrived[source]
        for peer in others:
            from_owner(me, peer).start()
        entering[me] = carries[me]

    @pl.when((turn >= 0) & (turn < owners))
    def _():
        for at in range(blocks):
            local_part(
                keep, turn, at, stream, inverse, feat, slope, weight, local, states, ends, product, powers
            )

        @pl.when(turn != me)
        def _():
            to_owner(me, turn).start()

    @pl.when(turn >= owners)
    def _():
        block = turn - owners

        @pl.when(block != me)
        def _():
            from_owner(block, me).wait_recv()

        for at in range(blocks):
            whole_part(
                keep, block, at, stream, inverse, feat, slope, local, states, entering, out, powers, result
            )

    @pl.when(turn == 2 * owners - 1)
    def _():
        for peer in others:

            @pl.when(peer < owners)
            def _():
                to_owner(me, peer).wait_send()

        @pl.when(me < owners)
        def _():
            for peer in others:
                from_owner(me, peer).wait_send()


def on_device(
    token_ids, embed_table, projected_table, feat_one, inner_taps, feat_two, decay, residue
):
    tokens = token_ids.shape[0]
    vocab, channels = embed_table.shape
    modes = decay.shape[1]
    count = lax.axis_size("ctx")
    peers = lax.axis_size("tp")
    steps = tokens // SEGMENTS
    keep = even(feat_two.shape[0] - 1)
    lead = even(keep + inner_taps.shape[0] - 1 + feat_one.shape[0] - 1)
    rows = (steps + keep) * SEGMENTS
    padded = -(-rows // LANES) * LANES
    earlier = lax.ppermute(token_ids, "ctx", [(source, source + 1) for source in range(count - 1)])
    feats = jnp.concatenate([feat_one, feat_two])
    rates = jnp.concatenate([jnp.transpose(decay), jnp.transpose(residue)])
    proj = jnp.transpose(projected_table, (1, 0, 2))

    wide = min(256, channels)
    blocks = channels // wide
    extended = (steps + lead) * SEGMENTS
    size = max(4 * LANES, channels // count)
    owners = channels // size
    begun = blocks + 1 + owners
    whole = lambda shape: pl.BlockSpec(shape, lambda c: (0,) * len(shape))
    raw = pltpu.VMEM((4, wide // LANES, extended, LANES), jnp.float32)
    shared = lambda number: pltpu.VMEM((number, modes, size), jnp.float32)
    return pl.pallas_call(
        functools.partial(kernel, lead, keep, count, peers, channels * peers),
        grid=(begun + owners,),
        in_specs=[
            whole((1, tokens)),
            whole((1, tokens)),
            pl.BlockSpec(memory_space=pl.ANY),
            pl.BlockSpec(memory_space=pl.ANY),
            whole(feats.shape),
            whole(inner_taps.shape),
            whole(rates.shape),
        ],
        out_specs=pl.BlockSpec((tokens, size), lambda c: (0, jnp.maximum(c - begun, 0))),
        out_shape=jax.ShapeDtypeStruct((tokens, channels), jnp.bfloat16),
        scratch_shapes=[
            pltpu.VMEM((channels // LANES, rows, LANES), jnp.bfloat16),
            pltpu.VMEM((SEGMENTS, padded), jnp.float32),
            raw,
            raw,
            pltpu.VMEM((padded, LANES), jnp.float32),
            pltpu.VMEM((LANES + tokens, LANES), jnp.float32),
            pltpu.VMEM((extended, vocab), jnp.bfloat16),
            pltpu.VMEM((blocks, 4, vocab, wide), jnp.bfloat16),
            pltpu.VMEM((padded, LANES), jnp.float32),
            pltpu.VMEM((peers, SEGMENTS, padded), jnp.float32),
            pltpu.VMEM((owners, size // LANES, tokens, LANES), jnp.float32),
            pltpu.VMEM((owners, size // LANES, modes, SEGMENTS, LANES), jnp.float32),
            shared(owners),
            shared(count),
            shared(count),
            shared(owners),
            pltpu.VMEM((tokens, LANES), jnp.float32),
            pltpu.VMEM((4, modes, LANES), jnp.float32),
            pltpu.VMEM((tokens, LANES), jnp.float32),
            pltpu.SemaphoreType.DMA((blocks, 2)),
            pltpu.SemaphoreType.DMA((peers,)),
            pltpu.SemaphoreType.DMA((peers,)),
        ]
        + [pltpu.SemaphoreType.DMA((count,))] * 4,
        compiler_params=pltpu.CompilerParams(
            dimension_semantics=("arbitrary",),
            collective_id=0,
            has_side_effects=True,
            vmem_limit_bytes=VMEM_LIMIT,
        ),
        name="hyena",
    )(
        earlier[None],
        token_ids[None],
        embed_table,
        proj,
        feats,
        inner_taps,
        rates,
    )


def solution(mesh):
    placed = (
        P("ctx"),
        P(None, "tp"),
        P(None, None, "tp"),
        P(None, None, "tp"),
        P(None, "tp"),
        P(None, None, "tp"),
        P("tp", None),
        P("tp", None),
    )
    return jax.shard_map(
        on_device, mesh=mesh, in_specs=placed, out_specs=P("ctx", "tp"), check_vma=False
    )
```

```python
import functools

import jax
import jax.numpy as jnp
from jax import lax
from jax.experimental import pallas as pl
from jax.experimental.pallas import tpu as pltpu
from jax.sharding import PartitionSpec as P

epsilon = 1e-06
HALO = 16
SEGMENTS = 8
LANES = 128
VMEM_LIMIT = 48 * 1024 * 1024
MESH = pl.DeviceIdType.MESH


def even(value):
    return value + value % 2


def wide_row(ref, index):
    return jnp.broadcast_to(ref[index], (SEGMENTS, LANES))


def lanes_of(block):
    return pl.ds(pl.multiple_of(block * LANES, LANES), LANES)


def weighted(taps, series):
    terms = [tap * value for tap, value in zip(taps, series)]
    total = terms[0]
    for term in terms[1:]:
        total = total + term
    return total


def tree_sum(terms):
    while len(terms) > 1:
        pairs = [a + b for a, b in zip(terms[::2], terms[1::2])]
        terms = pairs + terms[2 * len(pairs) :]
    return terms[0]


def first_part(
    turn,
    lead,
    keep,
    me,
    earlier,
    ids,
    embed,
    proj,
    feat,
    inner,
    stream,
    sums,
    raw_a,
    raw_b,
    squares,
    natural,
    one_hot,
    tables,
    arrival,
):
    groups, _, vocab, width = tables.shape
    blocks = width // LANES
    tokens = ids.shape[1]
    steps = tokens // SEGMENTS
    reach = feat.shape[0]
    span = inner.shape[0]

    def fetches(group):
        lanes = pl.ds(pl.multiple_of(group * width, LANES), width)
        return (
            pltpu.make_async_copy(
                embed.at[:, lanes], tables.at[group, 0], arrival.at[group, 0]
            ),
            pltpu.make_async_copy(
                proj.at[:, :, lanes], tables.at[group, pl.ds(1, 3)], arrival.at[group, 1]
            ),
        )

    def set_up():
        for group in range(groups):
            for fetch in fetches(group):
                fetch.start()
        squares[...] = jnp.zeros_like(squares)
        entry = lax.broadcasted_iota(jnp.int32, (2 * SEGMENTS, LANES), 1)

        def spread(at, piece):
            square = jnp.broadcast_to(piece.astype(jnp.float32), (LANES, LANES))
            natural[pl.ds(at, LANES), :] = jnp.transpose(square)

        def mark(first, last):
            for step in range(first, last, 2):
                rows = [
                    natural[pl.ds(LANES + step + k, SEGMENTS, stride=steps), :] for k in range(2)
                ]
                found = jnp.concatenate(rows, axis=0)
                where = pl.ds((step + lead) * SEGMENTS, 2 * SEGMENTS)
                for at in range(0, vocab, LANES):
                    equal = found == (entry + at).astype(jnp.float32)
                    one_hot[where, at : at + LANES] = jnp.where(equal, 1.0, 0.0).astype(
                        jnp.bfloat16
                    )

        for at in range(0, tokens, LANES):
            spread(LANES + at, ids[:, at : at + LANES])
        spread(0, jnp.where(me == 0, -1, earlier[:, tokens - LANES :]))
        mark(-lead, steps)

    def project(raw):
        both = jnp.dot(
            one_hot[...],
            jnp.concatenate([tables[turn, s] for s in range(4)], axis=1),
            preferred_element_type=jnp.float32,
        )
        for s in range(4):
            for block in range(blocks):
                at = (s * blocks + block) * LANES
                raw[s, block] = both[:, at : at + LANES]

    def mix(block, raw):
        place = (turn - 1) * blocks + block
        here = lanes_of(place)
        feat_taps = [
            [wide_row(feat, (j, slice(s, s + 1), here)) for j in range(reach)] for s in range(3)
        ]
        inner_taps = [wide_row(inner, (slice(j, j + 1), here)) for j in range(span)]

        def row(s, step):
            return raw[s, block, pl.ds((step + lead) * SEGMENTS, SEGMENTS), :]

        mixed = []
        held = []
        pasts = [[], [], []]
        for step in range(-lead, steps):
            for s in range(3):
                if s == 0 and step < 1 - keep - reach:
                    continue
                pasts[s] = ([row(s + 1, step)] + pasts[s])[:reach]
            if step < reach - 1 - lead:
                continue
            keyed = weighted(feat_taps[1], pasts[1])
            valued = weighted(feat_taps[2], pasts[2])
            mixed = ([keyed * valued] + mixed)[:span]
            if step < -keep:
                continue
            queries = weighted(feat_taps[0], pasts[0])
            total = row(0, step) + queries * weighted(inner_taps, mixed)
            at = step + keep
            squares[pl.ds(at * SEGMENTS, SEGMENTS), :] += total * total
            held.append(total)
            if len(held) == 2:
                pair = jnp.concatenate(held, axis=0).astype(jnp.bfloat16)
                stream[place, pl.ds((at - 1) * SEGMENTS, 2 * SEGMENTS), :] = pair
                held = []

    raws = (raw_a, raw_b)

    def mix_all(raw):
        for block in range(blocks):
            mix(block, raw)

    def work(parity):
        for fetch in fetches(turn):
            fetch.wait()
        mix_all(raws[1 - parity])
        project(raws[parity])

    @pl.when(turn == 0)
    def _():
        set_up()
        for fetch in fetches(0):
            fetch.wait()
        project(raw_a)

    for parity in range(2):

        @pl.when((turn > 0) & (turn < groups) & (turn % 2 == parity))
        def _():
            work(parity)

    @pl.when(turn == groups)
    def _():
        mix_all(raws[(groups - 1) % 2])
        sums[...] = lax.dot_general(
            jnp.ones((SEGMENTS, LANES), jnp.float32),
            squares[...],
            (((1,), (1,)), ((), ())),
            precision=lax.Precision.HIGHEST,
            preferred_element_type=jnp.float32,
        )


def norm_step(peers, channels, sums, inverse, parts, send, recv):
    me = lax.axis_index("tp")

    def copy(slot, peer):
        return pltpu.make_async_remote_copy(
            src_ref=sums,
            dst_ref=parts.at[slot],
            send_sem=send.at[peer],
            recv_sem=recv.at[slot],
            device_id={"tp": peer},
            device_id_type=MESH,
        )

    others = [lax.rem(me + k, peers) for k in range(1, peers)]
    for peer in others:
        copy(me, peer).start()
    parts[me] = sums[...]
    for peer in others:
        copy(peer, peer).wait_recv()
    total = parts[0]
    for k in range(1, peers):
        total = total + parts[k]
    row = lax.rsqrt(total / channels + epsilon)
    for at in range(0, inverse.shape[0], LANES):
        block = jnp.broadcast_to(row[0:1, at : at + LANES], (LANES, LANES))
        inverse[pl.ds(at, LANES), :] = jnp.transpose(block)
    for peer in others:
        copy(me, peer).wait_send()


def local_part(
    keep, block, at_lanes, stream, inverse, feat, slope, weight, local, states, ends, product, powers
):
    steps = stream.shape[1] // SEGMENTS - keep
    modes = slope.shape[0]
    reach = feat.shape[0]
    place = lax.broadcasted_iota(jnp.int32, (SEGMENTS, LANES), 0)
    lanes = slice(at_lanes * LANES, (at_lanes + 1) * LANES)
    place_at = block * (ends.shape[2] // LANES) + at_lanes
    here = lanes_of(place_at)
    taps = [[wide_row(feat, (j, slice(s, s + 1), here)) for j in range(reach)] for s in (1, 2)]

    def normed_pair(at):
        where = pl.ds(pl.multiple_of(at * SEGMENTS, 2 * SEGMENTS), 2 * SEGMENTS)
        both = stream[place_at, where, :].astype(jnp.float32) * inverse[where, :]
        return both[:SEGMENTS], both[SEGMENTS:]

    past = ()
    for at in range(keep - even(reach - 1), keep, 2):
        past = tuple(reversed(normed_pair(at))) + past
    past = past[: reach - 1]

    def multiply(pair, past):
        products = []
        for value in normed_pair(keep + 2 * pair):
            series = (value,) + past
            products.append(weighted(taps[0], series) * weighted(taps[1], series))
            past = series[: reach - 1]
        where = pl.ds(pl.multiple_of(pair * 2 * SEGMENTS, 2 * SEGMENTS), 2 * SEGMENTS)
        rounded = jnp.concatenate(products, axis=0).astype(jnp.bfloat16)
        product[where, :] = rounded.astype(jnp.float32)
        return past

    lax.fori_loop(0, steps // 2, multiply, past, unroll=16)

    powers[0] = jnp.exp(-slope[:, here])
    leap = jnp.exp(slope[:, here] * float(-steps))
    for level in range(1, 4):
        powers[level] = leap
        leap = leap * leap
    rates = [wide_row(powers, (0, slice(m, m + 1))) for m in range(modes)]
    weights = [wide_row(weight, (slice(m, m + 1), here)) for m in range(modes)]

    def step(at, held):
        where = pl.ds(pl.multiple_of(at * SEGMENTS, SEGMENTS), SEGMENTS)
        value = product[where, :]
        held = tuple(rates[m] * held[m] + weights[m] * value for m in range(modes))
        local[block, at_lanes, where, :] = tree_sum(list(held))
        return held

    zero = jnp.zeros((SEGMENTS, LANES), jnp.float32)
    held = lax.fori_loop(0, steps, step, (zero,) * modes, unroll=16)
    for m in range(modes):
        leaps = [wide_row(powers, (1 + level, slice(m, m + 1))) for level in range(3)]
        total = jnp.where(place >= 1, pltpu.roll(held[m], 1, 0), 0.0)
        for level in range(3):
            reaching = 1 << level
            moved = leaps[level] * pltpu.roll(total, reaching, 0)
            total = total + jnp.where(place >= reaching, moved, 0.0)
        states[block, at_lanes, m] = total
        ended = leaps[0] * total + held[m]
        ends[block, m : m + 1, lanes] = ended[SEGMENTS - 1 :]


def whole_part(
    keep, block, at_lanes, stream, inverse, feat, slope, local, states, entering, out, powers, result
):
    steps = stream.shape[1] // SEGMENTS - keep
    modes = slope.shape[0]
    reach = feat.shape[0]
    place = lax.broadcasted_iota(jnp.int32, (SEGMENTS, LANES), 0)
    ahead = (place * -steps - 1).astype(jnp.float32)
    lanes = slice(at_lanes * LANES, (at_lanes + 1) * LANES)
    place_at = block * (entering.shape[2] // LANES) + at_lanes
    here = lanes_of(place_at)
    taps = [wide_row(feat, (j, slice(0, 1), here)) for j in range(reach)]
    powers[0] = jnp.exp(-slope[:, here])
    rates = [wide_row(powers, (0, slice(m, m + 1))) for m in range(modes)]

    def wide_pair(at):
        where = pl.ds(pl.multiple_of(at * SEGMENTS, 2 * SEGMENTS), 2 * SEGMENTS)
        both = stream[place_at, where, :].astype(jnp.float32)
        normed = both * inverse[where, :]
        halves = (slice(0, SEGMENTS), slice(SEGMENTS, 2 * SEGMENTS))
        return [(both[half], normed[half]) for half in halves]

    past = ()
    for at in range(keep - even(reach - 1), keep, 2):
        past = tuple(normed for _, normed in reversed(wide_pair(at))) + past
    past = past[: reach - 1]

    first = []
    for m in range(modes):
        reached = jnp.exp(wide_row(slope, (slice(m, m + 1), here)) * ahead)
        arriving = wide_row(entering, (block, slice(m, m + 1), lanes))
        first.append(rates[m] * states[block, at_lanes, m] + reached * arriving)

    def step(pair, carried):
        past, held = carried
        for half, (wide, normed) in enumerate(wide_pair(keep + 2 * pair)):
            at = 2 * pair + half
            series = (normed,) + past
            past = series[: reach - 1]
            where = pl.ds(pl.multiple_of(at * SEGMENTS, SEGMENTS), SEGMENTS)
            convolved = tree_sum(list(held)) + local[block, at_lanes, where, :]
            result[pl.ds(at, SEGMENTS, stride=steps), :] = wide + weighted(taps, series) * convolved
            held = tuple(rates[m] * held[m] for m in range(modes))
        return past, held

    lax.fori_loop(0, steps // 2, step, (past, tuple(first)), unroll=8)
    out[:, lanes] = result[...].astype(jnp.bfloat16)


def kernel(
    lead,
    keep,
    count,
    peers,
    all_channels,
    earlier,
    ids,
    embed,
    proj,
    feats,
    inner,
    rates,
    out,
    stream,
    sums,
    raw_a,
    raw_b,
    squares,
    natural,
    one_hot,
    tables,
    inverse,
    parts,
    local,
    states,
    ends,
    arrived,
    carries,
    entering,
    product,
    powers,
    result,
    arrival,
    send_norm,
    recv_norm,
    send_out,
    recv_out,
    send_back,
    recv_back,
):
    reach = feats.shape[0] // 2
    feat_one, feat = feats.at[pl.ds(0, reach)], feats.at[pl.ds(reach, reach)]
    modes = rates.shape[0] // 2
    slope, weight = rates.at[pl.ds(0, modes)], rates.at[pl.ds(modes, modes)]
    now = pl.program_id(0)
    groups = tables.shape[0]
    turn = now - groups - 1
    me = lax.axis_index("ctx")
    owners, modes, width = ends.shape
    tokens = out.shape[0]
    blocks = width // LANES
    others = [lax.rem(me + k, count) for k in range(1, count)]

    barrier = pltpu.get_barrier_semaphore()

    @pl.when(now == 0)
    def _():
        for peer in others:
            pl.semaphore_signal(barrier, inc=1, device_id={"ctx": peer}, device_id_type=MESH)
        mine = lax.axis_index("tp")
        for k in range(1, peers):
            peer = lax.rem(mine + k, peers)
            pl.semaphore_signal(barrier, inc=1, device_id={"tp": peer}, device_id_type=MESH)

    first_part(
        now,
        lead,
        keep,
        me,
        earlier,
        ids,
        embed,
        proj,
        feat_one,
        inner,
        stream,
        sums,
        raw_a,
        raw_b,
        squares,
        natural,
        one_hot,
        tables,
        arrival,
    )

    @pl.when(now == groups)
    def _():
        pl.semaphore_wait(barrier, count - 1 + peers - 1)
        norm_step(peers, all_channels, sums, inverse, parts, send_norm, recv_norm)

    def to_owner(slot, owner):
        return pltpu.make_async_remote_copy(
            src_ref=ends.at[owner],
            dst_ref=arrived.at[slot],
            send_sem=send_out.at[owner],
            recv_sem=recv_out.at[slot],
            device_id={"ctx": owner},
            device_id_type=MESH,
        )

    def from_owner(slot, peer):
        return pltpu.make_async_remote_copy(
            src_ref=carries.at[peer],
            dst_ref=entering.at[slot],
            send_sem=send_back.at[peer],
            recv_sem=recv_back.at[slot],
            device_id={"ctx": peer},
            device_id_type=MESH,
        )

    @pl.when((turn == me + owners // 2) & (me < owners))
    def _():
        lanes = pl.ds(pl.multiple_of(me * width, LANES), width)
        leap = jnp.exp(slope[:, lanes] * float(-tokens))
        arrived[me] = ends[me]
        for peer in others:
            to_owner(peer, me).wait_recv()
        carry = jnp.zeros((modes, width), jnp.float32)
        for source in range(count):
            carries[source] = carry
            carry = leap * carry + arrived[source]
        for peer in others:
            from_owner(me, peer).start()
        entering[me] = carries[me]

    @pl.when((turn >= 0) & (turn < owners))
    def _():
        for at in range(blocks):
            local_part(
                keep, turn, at, stream, inverse, feat, slope, weight, local, states, ends, product, powers
            )

        @pl.when(turn != me)
        def _():
            to_owner(me, turn).start()

    @pl.when(turn >= owners)
    def _():
        block = turn - owners

        @pl.when(block != me)
        def _():
            from_owner(block, me).wait_recv()

        for at in range(blocks):
            whole_part(
                keep, block, at, stream, inverse, feat, slope, local, states, entering, out, powers, result
            )

    @pl.when(turn == 2 * owners - 1)
    def _():
        for peer in others:

            @pl.when(peer < owners)
            def _():
                to_owner(me, peer).wait_send()

        @pl.when(me < owners)
        def _():
            for peer in others:
                from_owner(me, peer).wait_send()


def on_device(
    token_ids, embed_table, projected_table, feat_one, inner_taps, feat_two, decay, residue
):
    tokens = token_ids.shape[0]
    vocab, channels = embed_table.shape
    modes = decay.shape[1]
    count = lax.axis_size("ctx")
    peers = lax.axis_size("tp")
    steps = tokens // SEGMENTS
    keep = even(feat_two.shape[0] - 1)
    lead = even(keep + inner_taps.shape[0] - 1 + feat_one.shape[0] - 1)
    rows = (steps + keep) * SEGMENTS
    padded = -(-rows // LANES) * LANES
    earlier = lax.ppermute(token_ids, "ctx", [(source, source + 1) for source in range(count - 1)])
    feats = jnp.concatenate([feat_one, feat_two])
    rates = jnp.concatenate([jnp.transpose(decay), jnp.transpose(residue)])
    proj = jnp.transpose(projected_table, (1, 0, 2))

    wide = min(512, channels)
    blocks = channels // wide
    extended = (steps + lead) * SEGMENTS
    size = max(4 * LANES, channels // count)
    owners = channels // size
    begun = blocks + 1 + owners
    whole = lambda shape: pl.BlockSpec(shape, lambda c: (0,) * len(shape))
    raw = pltpu.VMEM((4, wide // LANES, extended, LANES), jnp.float32)
    shared = lambda number: pltpu.VMEM((number, modes, size), jnp.float32)
    return pl.pallas_call(
        functools.partial(kernel, lead, keep, count, peers, channels * peers),
        grid=(begun + owners,),
        in_specs=[
            whole((1, tokens)),
            whole((1, tokens)),
            pl.BlockSpec(memory_space=pl.ANY),
            pl.BlockSpec(memory_space=pl.ANY),
            whole(feats.shape),
            whole(inner_taps.shape),
            whole(rates.shape),
        ],
        out_specs=pl.BlockSpec((tokens, size), lambda c: (0, jnp.maximum(c - begun, 0))),
        out_shape=jax.ShapeDtypeStruct((tokens, channels), jnp.bfloat16),
        scratch_shapes=[
            pltpu.VMEM((channels // LANES, rows, LANES), jnp.bfloat16),
            pltpu.VMEM((SEGMENTS, padded), jnp.float32),
            raw,
            raw,
            pltpu.VMEM((padded, LANES), jnp.float32),
            pltpu.VMEM((LANES + tokens, LANES), jnp.float32),
            pltpu.VMEM((extended, vocab), jnp.bfloat16),
            pltpu.VMEM((blocks, 4, vocab, wide), jnp.bfloat16),
            pltpu.VMEM((padded, LANES), jnp.float32),
            pltpu.VMEM((peers, SEGMENTS, padded), jnp.float32),
            pltpu.VMEM((owners, size // LANES, tokens, LANES), jnp.float32),
            pltpu.VMEM((owners, size // LANES, modes, SEGMENTS, LANES), jnp.float32),
            shared(owners),
            shared(count),
            shared(count),
            shared(owners),
            pltpu.VMEM((tokens, LANES), jnp.float32),
            pltpu.VMEM((4, modes, LANES), jnp.float32),
            pltpu.VMEM((tokens, LANES), jnp.float32),
            pltpu.SemaphoreType.DMA((blocks, 2)),
            pltpu.SemaphoreType.DMA((peers,)),
            pltpu.SemaphoreType.DMA((peers,)),
        ]
        + [pltpu.SemaphoreType.DMA((count,))] * 4,
        compiler_params=pltpu.CompilerParams(
            dimension_semantics=("arbitrary",),
            collective_id=0,
            has_side_effects=True,
            vmem_limit_bytes=VMEM_LIMIT,
        ),
        name="hyena",
    )(
        earlier[None],
        token_ids[None],
        embed_table,
        proj,
        feats,
        inner_taps,
        rates,
    )


def solution(mesh):
    placed = (
        P("ctx"),
        P(None, "tp"),
        P(None, None, "tp"),
        P(None, None, "tp"),
        P(None, "tp"),
        P(None, None, "tp"),
        P("tp", None),
        P("tp", None),
    )
    return jax.shard_map(
        on_device, mesh=mesh, in_specs=placed, out_specs=P("ctx", "tp"), check_vma=False
    )
```

```python
import functools

import jax
import jax.numpy as jnp
from jax import lax
from jax.experimental import pallas as pl
from jax.experimental.pallas import tpu as pltpu
from jax.sharding import PartitionSpec as P

epsilon = 1e-06
HALO = 16
SEGMENTS = 8
LANES = 128
VMEM_LIMIT = 48 * 1024 * 1024
MESH = pl.DeviceIdType.MESH


def even(value):
    return value + value % 2


def wide_row(ref, index):
    return jnp.broadcast_to(ref[index], (SEGMENTS, LANES))


def lanes_of(block):
    return pl.ds(pl.multiple_of(block * LANES, LANES), LANES)


def weighted(taps, series):
    terms = [tap * value for tap, value in zip(taps, series)]
    total = terms[0]
    for term in terms[1:]:
        total = total + term
    return total


def tree_sum(terms):
    while len(terms) > 1:
        pairs = [a + b for a, b in zip(terms[::2], terms[1::2])]
        terms = pairs + terms[2 * len(pairs) :]
    return terms[0]


def first_part(
    turn,
    lead,
    keep,
    me,
    earlier,
    ids,
    embed,
    proj,
    feat,
    inner,
    stream,
    sums,
    raw_a,
    raw_b,
    squares,
    natural,
    one_hot,
    tables,
    arrival,
):
    groups, _, vocab, width = tables.shape
    blocks = width // LANES
    tokens = ids.shape[1]
    steps = tokens // SEGMENTS
    reach = feat.shape[0]
    span = inner.shape[0]

    def fetches(group):
        lanes = pl.ds(pl.multiple_of(group * width, LANES), width)
        return (
            pltpu.make_async_copy(
                embed.at[:, lanes], tables.at[group, 0], arrival.at[group, 0]
            ),
            pltpu.make_async_copy(
                proj.at[:, :, lanes], tables.at[group, pl.ds(1, 3)], arrival.at[group, 1]
            ),
        )

    def set_up():
        for group in range(groups):
            for fetch in fetches(group):
                fetch.start()
        squares[...] = jnp.zeros_like(squares)
        entry = lax.broadcasted_iota(jnp.int32, (2 * SEGMENTS, LANES), 1)

        def spread(at, piece):
            square = jnp.broadcast_to(piece.astype(jnp.float32), (LANES, LANES))
            natural[pl.ds(at, LANES), :] = jnp.transpose(square)

        def mark(first, last):
            for step in range(first, last, 2):
                rows = [
                    natural[pl.ds(LANES + step + k, SEGMENTS, stride=steps), :] for k in range(2)
                ]
                found = jnp.concatenate(rows, axis=0)
                where = pl.ds((step + lead) * SEGMENTS, 2 * SEGMENTS)
                for at in range(0, vocab, LANES):
                    equal = found == (entry + at).astype(jnp.float32)
                    one_hot[where, at : at + LANES] = jnp.where(equal, 1.0, 0.0).astype(
                        jnp.bfloat16
                    )

        for at in range(0, tokens, LANES):
            spread(LANES + at, ids[:, at : at + LANES])
        spread(0, jnp.where(me == 0, -1, earlier[:, tokens - LANES :]))
        mark(-lead, steps)

    def project(raw):
        both = jnp.dot(
            one_hot[...],
            jnp.concatenate([tables[turn, s] for s in range(4)], axis=1),
            preferred_element_type=jnp.float32,
        )
        for s in range(4):
            for block in range(blocks):
                at = (s * blocks + block) * LANES
                raw[s, block] = both[:, at : at + LANES]

    def mix(block, raw):
        place = (turn - 1) * blocks + block
        here = lanes_of(place)
        feat_taps = [
            [wide_row(feat, (j, slice(s, s + 1), here)) for j in range(reach)] for s in range(3)
        ]
        inner_taps = [wide_row(inner, (slice(j, j + 1), here)) for j in range(span)]

        def row(s, step):
            return raw[s, block, pl.ds((step + lead) * SEGMENTS, SEGMENTS), :]

        mixed = []
        held = []
        pasts = [[], [], []]
        for step in range(-lead, steps):
            for s in range(3):
                if s == 0 and step < 1 - keep - reach:
                    continue
                pasts[s] = ([row(s + 1, step)] + pasts[s])[:reach]
            if step < reach - 1 - lead:
                continue
            keyed = weighted(feat_taps[1], pasts[1])
            valued = weighted(feat_taps[2], pasts[2])
            mixed = ([keyed * valued] + mixed)[:span]
            if step < -keep:
                continue
            queries = weighted(feat_taps[0], pasts[0])
            total = row(0, step) + queries * weighted(inner_taps, mixed)
            at = step + keep
            squares[pl.ds(at * SEGMENTS, SEGMENTS), :] += total * total
            held.append(total)
            if len(held) == 2:
                pair = jnp.concatenate(held, axis=0).astype(jnp.bfloat16)
                stream[place, pl.ds((at - 1) * SEGMENTS, 2 * SEGMENTS), :] = pair
                held = []

    raws = (raw_a, raw_b)

    def mix_all(raw):
        for block in range(blocks):
            mix(block, raw)

    def work(parity):
        for fetch in fetches(turn):
            fetch.wait()
        mix_all(raws[1 - parity])
        project(raws[parity])

    @pl.when(turn == 0)
    def _():
        set_up()
        for fetch in fetches(0):
            fetch.wait()
        project(raw_a)

    for parity in range(2):

        @pl.when((turn > 0) & (turn < groups) & (turn % 2 == parity))
        def _():
            work(parity)

    @pl.when(turn == groups)
    def _():
        mix_all(raws[(groups - 1) % 2])
        sums[...] = lax.dot_general(
            jnp.ones((SEGMENTS, LANES), jnp.float32),
            squares[...],
            (((1,), (1,)), ((), ())),
            precision=lax.Precision.HIGHEST,
            preferred_element_type=jnp.float32,
        )


def norm_step(peers, channels, sums, inverse, parts, send, recv):
    me = lax.axis_index("tp")

    def copy(slot, peer):
        return pltpu.make_async_remote_copy(
            src_ref=sums,
            dst_ref=parts.at[slot],
            send_sem=send.at[peer],
            recv_sem=recv.at[slot],
            device_id={"tp": peer},
            device_id_type=MESH,
        )

    others = [lax.rem(me + k, peers) for k in range(1, peers)]
    for peer in others:
        copy(me, peer).start()
    parts[me] = sums[...]
    for peer in others:
        copy(peer, peer).wait_recv()
    total = parts[0]
    for k in range(1, peers):
        total = total + parts[k]
    row = lax.rsqrt(total / channels + epsilon)
    for at in range(0, inverse.shape[0], LANES):
        block = jnp.broadcast_to(row[0:1, at : at + LANES], (LANES, LANES))
        inverse[pl.ds(at, LANES), :] = jnp.transpose(block)
    for peer in others:
        copy(me, peer).wait_send()


def local_part(
    keep, block, at_lanes, stream, inverse, feat, slope, weight, local, states, ends, product, powers
):
    steps = stream.shape[1] // SEGMENTS - keep
    modes = slope.shape[0]
    reach = feat.shape[0]
    place = lax.broadcasted_iota(jnp.int32, (SEGMENTS, LANES), 0)
    lanes = slice(at_lanes * LANES, (at_lanes + 1) * LANES)
    place_at = block * (ends.shape[2] // LANES) + at_lanes
    here = lanes_of(place_at)
    taps = [[wide_row(feat, (j, slice(s, s + 1), here)) for j in range(reach)] for s in (1, 2)]

    def normed_pair(at):
        where = pl.ds(pl.multiple_of(at * SEGMENTS, 2 * SEGMENTS), 2 * SEGMENTS)
        both = stream[place_at, where, :].astype(jnp.float32) * inverse[where, :]
        return both[:SEGMENTS], both[SEGMENTS:]

    past = ()
    for at in range(keep - even(reach - 1), keep, 2):
        past = tuple(reversed(normed_pair(at))) + past
    past = past[: reach - 1]

    def multiply(pair, past):
        products = []
        for value in normed_pair(keep + 2 * pair):
            series = (value,) + past
            products.append(weighted(taps[0], series) * weighted(taps[1], series))
            past = series[: reach - 1]
        where = pl.ds(pl.multiple_of(pair * 2 * SEGMENTS, 2 * SEGMENTS), 2 * SEGMENTS)
        rounded = jnp.concatenate(products, axis=0).astype(jnp.bfloat16)
        product[where, :] = rounded.astype(jnp.float32)
        return past

    lax.fori_loop(0, steps // 2, multiply, past, unroll=16)

    powers[0] = jnp.exp(-slope[:, here])
    leap = jnp.exp(slope[:, here] * float(-steps))
    for level in range(1, 4):
        powers[level] = leap
        leap = leap * leap
    rates = [wide_row(powers, (0, slice(m, m + 1))) for m in range(modes)]
    weights = [wide_row(weight, (slice(m, m + 1), here)) for m in range(modes)]

    def step(at, held):
        where = pl.ds(pl.multiple_of(at * SEGMENTS, SEGMENTS), SEGMENTS)
        value = product[where, :]
        held = tuple(rates[m] * held[m] + weights[m] * value for m in range(modes))
        local[block, at_lanes, where, :] = tree_sum(list(held))
        return held

    zero = jnp.zeros((SEGMENTS, LANES), jnp.float32)
    held = lax.fori_loop(0, steps, step, (zero,) * modes, unroll=32)
    for m in range(modes):
        leaps = [wide_row(powers, (1 + level, slice(m, m + 1))) for level in range(3)]
        total = jnp.where(place >= 1, pltpu.roll(held[m], 1, 0), 0.0)
        for level in range(3):
            reaching = 1 << level
            moved = leaps[level] * pltpu.roll(total, reaching, 0)
            total = total + jnp.where(place >= reaching, moved, 0.0)
        states[block, at_lanes, m] = total
        ended = leaps[0] * total + held[m]
        ends[block, m : m + 1, lanes] = ended[SEGMENTS - 1 :]


def whole_part(
    keep, block, at_lanes, stream, inverse, feat, slope, local, states, entering, out, powers, result
):
    steps = stream.shape[1] // SEGMENTS - keep
    modes = slope.shape[0]
    reach = feat.shape[0]
    place = lax.broadcasted_iota(jnp.int32, (SEGMENTS, LANES), 0)
    ahead = (place * -steps - 1).astype(jnp.float32)
    lanes = slice(at_lanes * LANES, (at_lanes + 1) * LANES)
    place_at = block * (entering.shape[2] // LANES) + at_lanes
    here = lanes_of(place_at)
    taps = [wide_row(feat, (j, slice(0, 1), here)) for j in range(reach)]
    powers[0] = jnp.exp(-slope[:, here])
    rates = [wide_row(powers, (0, slice(m, m + 1))) for m in range(modes)]

    def wide_pair(at):
        where = pl.ds(pl.multiple_of(at * SEGMENTS, 2 * SEGMENTS), 2 * SEGMENTS)
        both = stream[place_at, where, :].astype(jnp.float32)
        normed = both * inverse[where, :]
        halves = (slice(0, SEGMENTS), slice(SEGMENTS, 2 * SEGMENTS))
        return [(both[half], normed[half]) for half in halves]

    past = ()
    for at in range(keep - even(reach - 1), keep, 2):
        past = tuple(normed for _, normed in reversed(wide_pair(at))) + past
    past = past[: reach - 1]

    first = []
    for m in range(modes):
        reached = jnp.exp(wide_row(slope, (slice(m, m + 1), here)) * ahead)
        arriving = wide_row(entering, (block, slice(m, m + 1), lanes))
        first.append(rates[m] * states[block, at_lanes, m] + reached * arriving)

    def step(pair, carried):
        past, held = carried
        for half, (wide, normed) in enumerate(wide_pair(keep + 2 * pair)):
            at = 2 * pair + half
            series = (normed,) + past
            past = series[: reach - 1]
            where = pl.ds(pl.multiple_of(at * SEGMENTS, SEGMENTS), SEGMENTS)
            convolved = tree_sum(list(held)) + local[block, at_lanes, where, :]
            result[pl.ds(at, SEGMENTS, stride=steps), :] = wide + weighted(taps, series) * convolved
            held = tuple(rates[m] * held[m] for m in range(modes))
        return past, held

    lax.fori_loop(0, steps // 2, step, (past, tuple(first)), unroll=16)
    out[:, lanes] = result[...].astype(jnp.bfloat16)


def kernel(
    lead,
    keep,
    count,
    peers,
    all_channels,
    modes,
    earlier,
    ids,
    embed,
    proj,
    feats,
    rates,
    out,
    stream,
    sums,
    raw_a,
    raw_b,
    squares,
    natural,
    one_hot,
    tables,
    inverse,
    parts,
    local,
    states,
    ends,
    arrived,
    carries,
    entering,
    product,
    powers,
    result,
    arrival,
    send_norm,
    recv_norm,
    send_out,
    recv_out,
    send_back,
    recv_back,
):
    reach = feats.shape[0] // 2
    feat_one, feat = feats.at[pl.ds(0, reach)], feats.at[pl.ds(reach, reach)]
    slope, weight = rates.at[pl.ds(0, modes)], rates.at[pl.ds(modes, modes)]
    inner = rates.at[pl.ds(2 * modes, rates.shape[0] - 2 * modes)]
    now = pl.program_id(0)
    groups = tables.shape[0]
    turn = now - groups - 1
    me = lax.axis_index("ctx")
    owners, modes, width = ends.shape
    tokens = out.shape[0]
    blocks = width // LANES
    others = [lax.rem(me + k, count) for k in range(1, count)]

    barrier = pltpu.get_barrier_semaphore()

    @pl.when(now == 0)
    def _():
        for peer in others:
            pl.semaphore_signal(barrier, inc=1, device_id={"ctx": peer}, device_id_type=MESH)
        mine = lax.axis_index("tp")
        for k in range(1, peers):
            peer = lax.rem(mine + k, peers)
            pl.semaphore_signal(barrier, inc=1, device_id={"tp": peer}, device_id_type=MESH)

    first_part(
        now,
        lead,
        keep,
        me,
        earlier,
        ids,
        embed,
        proj,
        feat_one,
        inner,
        stream,
        sums,
        raw_a,
        raw_b,
        squares,
        natural,
        one_hot,
        tables,
        arrival,
    )

    @pl.when(now == groups)
    def _():
        pl.semaphore_wait(barrier, count - 1 + peers - 1)
        norm_step(peers, all_channels, sums, inverse, parts, send_norm, recv_norm)

    def to_owner(slot, owner):
        return pltpu.make_async_remote_copy(
            src_ref=ends.at[owner],
            dst_ref=arrived.at[slot],
            send_sem=send_out.at[owner],
            recv_sem=recv_out.at[slot],
            device_id={"ctx": owner},
            device_id_type=MESH,
        )

    def from_owner(slot, peer):
        return pltpu.make_async_remote_copy(
            src_ref=carries.at[peer],
            dst_ref=entering.at[slot],
            send_sem=send_back.at[peer],
            recv_sem=recv_back.at[slot],
            device_id={"ctx": peer},
            device_id_type=MESH,
        )

    @pl.when((turn == me + owners // 2) & (me < owners))
    def _():
        lanes = pl.ds(pl.multiple_of(me * width, LANES), width)
        leap = jnp.exp(slope[:, lanes] * float(-tokens))
        arrived[me] = ends[me]
        for peer in others:
            to_owner(peer, me).wait_recv()
        carry = jnp.zeros((modes, width), jnp.float32)
        for source in range(count):
            carries[source] = carry
            carry = leap * carry + arrived[source]
        for peer in others:
            from_owner(me, peer).start()
        entering[me] = carries[me]

    @pl.when((turn >= 0) & (turn < owners))
    def _():
        for at in range(blocks):
            local_part(
                keep, turn, at, stream, inverse, feat, slope, weight, local, states, ends, product, powers
            )

        @pl.when(turn != me)
        def _():
            to_owner(me, turn).start()

    @pl.when(turn >= owners)
    def _():
        block = turn - owners

        @pl.when(block != me)
        def _():
            from_owner(block, me).wait_recv()

        for at in range(blocks):
            whole_part(
                keep, block, at, stream, inverse, feat, slope, local, states, entering, out, powers, result
            )

    @pl.when(turn == 2 * owners - 1)
    def _():
        for peer in others:

            @pl.when(peer < owners)
            def _():
                to_owner(me, peer).wait_send()

        @pl.when(me < owners)
        def _():
            for peer in others:
                from_owner(me, peer).wait_send()


def on_device(
    token_ids, embed_table, projected_table, feat_one, inner_taps, feat_two, decay, residue
):
    tokens = token_ids.shape[0]
    vocab, channels = embed_table.shape
    modes = decay.shape[1]
    count = lax.axis_size("ctx")
    peers = lax.axis_size("tp")
    steps = tokens // SEGMENTS
    keep = even(feat_two.shape[0] - 1)
    lead = even(keep + inner_taps.shape[0] - 1 + feat_one.shape[0] - 1)
    rows = (steps + keep) * SEGMENTS
    padded = -(-rows // LANES) * LANES
    earlier = lax.ppermute(token_ids, "ctx", [(source, source + 1) for source in range(count - 1)])
    feats = jnp.concatenate([feat_one, feat_two])
    rates = jnp.concatenate([jnp.transpose(decay), jnp.transpose(residue), inner_taps])
    proj = jnp.transpose(projected_table, (1, 0, 2))

    wide = min(512, channels)
    blocks = channels // wide
    extended = (steps + lead) * SEGMENTS
    size = max(4 * LANES, channels // count)
    owners = channels // size
    begun = blocks + 1 + owners
    whole = lambda shape: pl.BlockSpec(shape, lambda c: (0,) * len(shape))
    raw = pltpu.VMEM((4, wide // LANES, extended, LANES), jnp.float32)
    shared = lambda number: pltpu.VMEM((number, modes, size), jnp.float32)
    return pl.pallas_call(
        functools.partial(kernel, lead, keep, count, peers, channels * peers, modes),
        grid=(begun + owners,),
        in_specs=[
            whole((1, tokens)),
            whole((1, tokens)),
            pl.BlockSpec(memory_space=pl.ANY),
            pl.BlockSpec(memory_space=pl.ANY),
            whole(feats.shape),
            whole(rates.shape),
        ],
        out_specs=pl.BlockSpec((tokens, size), lambda c: (0, jnp.maximum(c - begun, 0))),
        out_shape=jax.ShapeDtypeStruct((tokens, channels), jnp.bfloat16),
        scratch_shapes=[
            pltpu.VMEM((channels // LANES, rows, LANES), jnp.bfloat16),
            pltpu.VMEM((SEGMENTS, padded), jnp.float32),
            raw,
            raw,
            pltpu.VMEM((padded, LANES), jnp.float32),
            pltpu.VMEM((LANES + tokens, LANES), jnp.float32),
            pltpu.VMEM((extended, vocab), jnp.bfloat16),
            pltpu.VMEM((blocks, 4, vocab, wide), jnp.bfloat16),
            pltpu.VMEM((padded, LANES), jnp.float32),
            pltpu.VMEM((peers, SEGMENTS, padded), jnp.float32),
            pltpu.VMEM((owners, size // LANES, tokens, LANES), jnp.float32),
            pltpu.VMEM((owners, size // LANES, modes, SEGMENTS, LANES), jnp.float32),
            shared(owners),
            shared(count),
            shared(count),
            shared(owners),
            pltpu.VMEM((tokens, LANES), jnp.float32),
            pltpu.VMEM((4, modes, LANES), jnp.float32),
            pltpu.VMEM((tokens, LANES), jnp.float32),
            pltpu.SemaphoreType.DMA((blocks, 2)),
            pltpu.SemaphoreType.DMA((peers,)),
            pltpu.SemaphoreType.DMA((peers,)),
        ]
        + [pltpu.SemaphoreType.DMA((count,))] * 4,
        compiler_params=pltpu.CompilerParams(
            dimension_semantics=("arbitrary",),
            collective_id=0,
            has_side_effects=True,
            vmem_limit_bytes=VMEM_LIMIT,
        ),
        name="hyena",
    )(
        earlier[None],
        token_ids[None],
        embed_table,
        proj,
        feats,
        rates,
    )


def solution(mesh):
    placed = (
        P("ctx"),
        P(None, "tp"),
        P(None, None, "tp"),
        P(None, None, "tp"),
        P(None, "tp"),
        P(None, None, "tp"),
        P("tp", None),
        P("tp", None),
    )
    return jax.shard_map(
        on_device, mesh=mesh, in_specs=placed, out_specs=P("ctx", "tp"), check_vma=False
    )
```

```python
import functools

import jax
import jax.numpy as jnp
from jax import lax
from jax.experimental import pallas as pl
from jax.experimental.pallas import tpu as pltpu
from jax.sharding import PartitionSpec as P

epsilon = 1e-06
HALO = 16
SEGMENTS = 8
LANES = 128
VMEM_LIMIT = 48 * 1024 * 1024
MESH = pl.DeviceIdType.MESH


def even(value):
    return value + value % 2


def wide_row(ref, index):
    return jnp.broadcast_to(ref[index], (SEGMENTS, LANES))


def lanes_of(block):
    return pl.ds(pl.multiple_of(block * LANES, LANES), LANES)


def weighted(taps, series):
    terms = [tap * value for tap, value in zip(taps, series)]
    total = terms[0]
    for term in terms[1:]:
        total = total + term
    return total


def tree_sum(terms):
    while len(terms) > 1:
        pairs = [a + b for a, b in zip(terms[::2], terms[1::2])]
        terms = pairs + terms[2 * len(pairs) :]
    return terms[0]


def first_part(
    turn,
    lead,
    keep,
    me,
    earlier,
    ids,
    embed,
    proj,
    feat,
    inner,
    stream,
    sums,
    raw_a,
    raw_b,
    squares,
    natural,
    one_hot,
    tables,
    arrival,
):
    groups, _, vocab, width = tables.shape
    blocks = width // LANES
    tokens = ids.shape[1]
    steps = tokens // SEGMENTS
    reach = feat.shape[0]
    span = inner.shape[0]

    def fetches(group):
        lanes = pl.ds(pl.multiple_of(group * width, LANES), width)
        return (
            pltpu.make_async_copy(
                embed.at[:, lanes], tables.at[group, 0], arrival.at[group, 0]
            ),
            pltpu.make_async_copy(
                proj.at[:, :, lanes], tables.at[group, pl.ds(1, 3)], arrival.at[group, 1]
            ),
        )

    def set_up():
        for group in range(groups):
            for fetch in fetches(group):
                fetch.start()
        squares[...] = jnp.zeros_like(squares)
        entry = lax.broadcasted_iota(jnp.int32, (2 * SEGMENTS, LANES), 1)

        def spread(at, piece):
            square = jnp.broadcast_to(piece.astype(jnp.float32), (LANES, LANES))
            natural[pl.ds(at, LANES), :] = jnp.transpose(square)

        def mark(first, last):
            for step in range(first, last, 2):
                rows = [
                    natural[pl.ds(LANES + step + k, SEGMENTS, stride=steps), :] for k in range(2)
                ]
                found = jnp.concatenate(rows, axis=0)
                where = pl.ds((step + lead) * SEGMENTS, 2 * SEGMENTS)
                for at in range(0, vocab, LANES):
                    equal = found == (entry + at).astype(jnp.float32)
                    one_hot[where, at : at + LANES] = jnp.where(equal, 1.0, 0.0).astype(
                        jnp.bfloat16
                    )

        for at in range(0, tokens, LANES):
            spread(LANES + at, ids[:, at : at + LANES])
        spread(0, jnp.where(me == 0, -1, earlier[:, tokens - LANES :]))
        mark(-lead, steps)

    def project(raw):
        both = jnp.dot(
            one_hot[...],
            jnp.concatenate([tables[turn, s] for s in range(4)], axis=1),
            preferred_element_type=jnp.float32,
        )
        for s in range(4):
            for block in range(blocks):
                at = (s * blocks + block) * LANES
                raw[s, block] = both[:, at : at + LANES]

    def mix(block, raw):
        place = (turn - 1) * blocks + block
        here = lanes_of(place)
        feat_taps = [
            [wide_row(feat, (j, slice(s, s + 1), here)) for j in range(reach)] for s in range(3)
        ]
        inner_taps = [wide_row(inner, (slice(j, j + 1), here)) for j in range(span)]

        def row(s, step):
            return raw[s, block, pl.ds((step + lead) * SEGMENTS, SEGMENTS), :]

        mixed = []
        held = []
        pasts = [[], [], []]
        for step in range(-lead, steps):
            for s in range(3):
                if s == 0 and step < 1 - keep - reach:
                    continue
                pasts[s] = ([row(s + 1, step)] + pasts[s])[:reach]
            if step < reach - 1 - lead:
                continue
            keyed = weighted(feat_taps[1], pasts[1])
            valued = weighted(feat_taps[2], pasts[2])
            mixed = ([keyed * valued] + mixed)[:span]
            if step < -keep:
                continue
            queries = weighted(feat_taps[0], pasts[0])
            total = row(0, step) + queries * weighted(inner_taps, mixed)
            at = step + keep
            squares[pl.ds(at * SEGMENTS, SEGMENTS), :] += total * total
            held.append(total)
            if len(held) == 2:
                pair = jnp.concatenate(held, axis=0).astype(jnp.bfloat16)
                stream[place, pl.ds((at - 1) * SEGMENTS, 2 * SEGMENTS), :] = pair
                held = []

    raws = (raw_a, raw_b)

    def mix_all(raw):
        for block in range(blocks):
            mix(block, raw)

    def work(parity):
        for fetch in fetches(turn):
            fetch.wait()
        mix_all(raws[1 - parity])
        project(raws[parity])

    @pl.when(turn == 0)
    def _():
        set_up()
        for fetch in fetches(0):
            fetch.wait()
        project(raw_a)

    for parity in range(2):

        @pl.when((turn > 0) & (turn < groups) & (turn % 2 == parity))
        def _():
            work(parity)

    @pl.when(turn == groups)
    def _():
        mix_all(raws[(groups - 1) % 2])
        sums[...] = lax.dot_general(
            jnp.ones((SEGMENTS, LANES), jnp.float32),
            squares[...],
            (((1,), (1,)), ((), ())),
            precision=lax.Precision.HIGHEST,
            preferred_element_type=jnp.float32,
        )


def norm_step(peers, channels, sums, inverse, parts, send, recv):
    me = lax.axis_index("tp")

    def copy(slot, peer):
        return pltpu.make_async_remote_copy(
            src_ref=sums,
            dst_ref=parts.at[slot],
            send_sem=send.at[peer],
            recv_sem=recv.at[slot],
            device_id={"tp": peer},
            device_id_type=MESH,
        )

    others = [lax.rem(me + k, peers) for k in range(1, peers)]
    for peer in others:
        copy(me, peer).start()
    parts[me] = sums[...]
    for peer in others:
        copy(peer, peer).wait_recv()
    total = parts[0]
    for k in range(1, peers):
        total = total + parts[k]
    row = lax.rsqrt(total / channels + epsilon)
    for at in range(0, inverse.shape[0], LANES):
        block = jnp.broadcast_to(row[0:1, at : at + LANES], (LANES, LANES))
        inverse[pl.ds(at, LANES), :] = jnp.transpose(block)
    for peer in others:
        copy(me, peer).wait_send()


def local_part(
    keep, block, at_lanes, stream, inverse, feat, slope, weight, local, states, ends, product, powers
):
    steps = stream.shape[1] // SEGMENTS - keep
    modes = slope.shape[0]
    reach = feat.shape[0]
    place = lax.broadcasted_iota(jnp.int32, (SEGMENTS, LANES), 0)
    lanes = slice(at_lanes * LANES, (at_lanes + 1) * LANES)
    place_at = block * (ends.shape[2] // LANES) + at_lanes
    here = lanes_of(place_at)
    taps = [[wide_row(feat, (j, slice(s, s + 1), here)) for j in range(reach)] for s in (1, 2)]

    def normed_pair(at):
        where = pl.ds(pl.multiple_of(at * SEGMENTS, 2 * SEGMENTS), 2 * SEGMENTS)
        both = stream[place_at, where, :].astype(jnp.float32) * inverse[where, :]
        return both[:SEGMENTS], both[SEGMENTS:]

    past = ()
    for at in range(keep - even(reach - 1), keep, 2):
        past = tuple(reversed(normed_pair(at))) + past
    past = past[: reach - 1]

    def multiply(pair, past):
        products = []
        for value in normed_pair(keep + 2 * pair):
            series = (value,) + past
            products.append(weighted(taps[0], series) * weighted(taps[1], series))
            past = series[: reach - 1]
        where = pl.ds(pl.multiple_of(pair * 2 * SEGMENTS, 2 * SEGMENTS), 2 * SEGMENTS)
        rounded = jnp.concatenate(products, axis=0).astype(jnp.bfloat16)
        product[where, :] = rounded.astype(jnp.float32)
        return past

    lax.fori_loop(0, steps // 2, multiply, past, unroll=32)

    powers[0] = jnp.exp(-slope[:, here])
    leap = jnp.exp(slope[:, here] * float(-steps))
    for level in range(1, 4):
        powers[level] = leap
        leap = leap * leap
    rates = [wide_row(powers, (0, slice(m, m + 1))) for m in range(modes)]
    weights = [wide_row(weight, (slice(m, m + 1), here)) for m in range(modes)]

    def step(at, held):
        where = pl.ds(pl.multiple_of(at * SEGMENTS, SEGMENTS), SEGMENTS)
        value = product[where, :]
        held = tuple(rates[m] * held[m] + weights[m] * value for m in range(modes))
        local[block, at_lanes, where, :] = tree_sum(list(held))
        return held

    zero = jnp.zeros((SEGMENTS, LANES), jnp.float32)
    held = lax.fori_loop(0, steps, step, (zero,) * modes, unroll=64)
    for m in range(modes):
        leaps = [wide_row(powers, (1 + level, slice(m, m + 1))) for level in range(3)]
        total = jnp.where(place >= 1, pltpu.roll(held[m], 1, 0), 0.0)
        for level in range(3):
            reaching = 1 << level
            moved = leaps[level] * pltpu.roll(total, reaching, 0)
            total = total + jnp.where(place >= reaching, moved, 0.0)
        states[block, at_lanes, m] = total
        ended = leaps[0] * total + held[m]
        ends[block, m : m + 1, lanes] = ended[SEGMENTS - 1 :]


def whole_part(
    keep, block, at_lanes, stream, inverse, feat, slope, local, states, entering, out, powers, result
):
    steps = stream.shape[1] // SEGMENTS - keep
    modes = slope.shape[0]
    reach = feat.shape[0]
    place = lax.broadcasted_iota(jnp.int32, (SEGMENTS, LANES), 0)
    ahead = (place * -steps - 1).astype(jnp.float32)
    lanes = slice(at_lanes * LANES, (at_lanes + 1) * LANES)
    place_at = block * (entering.shape[2] // LANES) + at_lanes
    here = lanes_of(place_at)
    taps = [wide_row(feat, (j, slice(0, 1), here)) for j in range(reach)]
    powers[0] = jnp.exp(-slope[:, here])
    rates = [wide_row(powers, (0, slice(m, m + 1))) for m in range(modes)]

    def wide_pair(at):
        where = pl.ds(pl.multiple_of(at * SEGMENTS, 2 * SEGMENTS), 2 * SEGMENTS)
        both = stream[place_at, where, :].astype(jnp.float32)
        normed = both * inverse[where, :]
        halves = (slice(0, SEGMENTS), slice(SEGMENTS, 2 * SEGMENTS))
        return [(both[half], normed[half]) for half in halves]

    past = ()
    for at in range(keep - even(reach - 1), keep, 2):
        past = tuple(normed for _, normed in reversed(wide_pair(at))) + past
    past = past[: reach - 1]

    first = []
    for m in range(modes):
        reached = jnp.exp(wide_row(slope, (slice(m, m + 1), here)) * ahead)
        arriving = wide_row(entering, (block, slice(m, m + 1), lanes))
        first.append(rates[m] * states[block, at_lanes, m] + reached * arriving)

    def step(pair, carried):
        past, held = carried
        for half, (wide, normed) in enumerate(wide_pair(keep + 2 * pair)):
            at = 2 * pair + half
            series = (normed,) + past
            past = series[: reach - 1]
            where = pl.ds(pl.multiple_of(at * SEGMENTS, SEGMENTS), SEGMENTS)
            convolved = tree_sum(list(held)) + local[block, at_lanes, where, :]
            result[pl.ds(at, SEGMENTS, stride=steps), :] = wide + weighted(taps, series) * convolved
            held = tuple(rates[m] * held[m] for m in range(modes))
        return past, held

    lax.fori_loop(0, steps // 2, step, (past, tuple(first)), unroll=32)
    out[:, lanes] = result[...].astype(jnp.bfloat16)


def kernel(
    lead,
    keep,
    count,
    peers,
    all_channels,
    modes,
    earlier,
    ids,
    embed,
    proj,
    feats,
    rates,
    out,
    stream,
    sums,
    raw_a,
    raw_b,
    squares,
    natural,
    one_hot,
    tables,
    inverse,
    parts,
    local,
    states,
    ends,
    arrived,
    carries,
    entering,
    product,
    powers,
    result,
    arrival,
    send_norm,
    recv_norm,
    send_out,
    recv_out,
    send_back,
    recv_back,
):
    reach = feats.shape[0] // 2
    feat_one, feat = feats.at[pl.ds(0, reach)], feats.at[pl.ds(reach, reach)]
    slope, weight = rates.at[pl.ds(0, modes)], rates.at[pl.ds(modes, modes)]
    inner = rates.at[pl.ds(2 * modes, rates.shape[0] - 2 * modes)]
    now = pl.program_id(0)
    groups = tables.shape[0]
    turn = now - groups - 1
    me = lax.axis_index("ctx")
    owners, modes, width = ends.shape
    tokens = out.shape[0]
    blocks = width // LANES
    others = [lax.rem(me + k, count) for k in range(1, count)]

    barrier = pltpu.get_barrier_semaphore()

    @pl.when(now == 0)
    def _():
        for peer in others:
            pl.semaphore_signal(barrier, inc=1, device_id={"ctx": peer}, device_id_type=MESH)
        mine = lax.axis_index("tp")
        for k in range(1, peers):
            peer = lax.rem(mine + k, peers)
            pl.semaphore_signal(barrier, inc=1, device_id={"tp": peer}, device_id_type=MESH)

    first_part(
        now,
        lead,
        keep,
        me,
        earlier,
        ids,
        embed,
        proj,
        feat_one,
        inner,
        stream,
        sums,
        raw_a,
        raw_b,
        squares,
        natural,
        one_hot,
        tables,
        arrival,
    )

    @pl.when(now == groups)
    def _():
        pl.semaphore_wait(barrier, count - 1 + peers - 1)
        norm_step(peers, all_channels, sums, inverse, parts, send_norm, recv_norm)

    def to_owner(slot, owner):
        return pltpu.make_async_remote_copy(
            src_ref=ends.at[owner],
            dst_ref=arrived.at[slot],
            send_sem=send_out.at[owner],
            recv_sem=recv_out.at[slot],
            device_id={"ctx": owner},
            device_id_type=MESH,
        )

    def from_owner(slot, peer):
        return pltpu.make_async_remote_copy(
            src_ref=carries.at[peer],
            dst_ref=entering.at[slot],
            send_sem=send_back.at[peer],
            recv_sem=recv_back.at[slot],
            device_id={"ctx": peer},
            device_id_type=MESH,
        )

    @pl.when((turn == me + owners // 2) & (me < owners))
    def _():
        lanes = pl.ds(pl.multiple_of(me * width, LANES), width)
        leap = jnp.exp(slope[:, lanes] * float(-tokens))
        arrived[me] = ends[me]
        for peer in others:
            to_owner(peer, me).wait_recv()
        carry = jnp.zeros((modes, width), jnp.float32)
        for source in range(count):
            carries[source] = carry
            carry = leap * carry + arrived[source]
        for peer in others:
            from_owner(me, peer).start()
        entering[me] = carries[me]

    @pl.when((turn >= 0) & (turn < owners))
    def _():
        for at in range(blocks):
            local_part(
                keep, turn, at, stream, inverse, feat, slope, weight, local, states, ends, product, powers
            )

        @pl.when(turn != me)
        def _():
            to_owner(me, turn).start()

    @pl.when(turn >= owners)
    def _():
        block = turn - owners

        @pl.when(block != me)
        def _():
            from_owner(block, me).wait_recv()

        for at in range(blocks):
            whole_part(
                keep, block, at, stream, inverse, feat, slope, local, states, entering, out, powers, result
            )

    @pl.when(turn == 2 * owners - 1)
    def _():
        for peer in others:

            @pl.when(peer < owners)
            def _():
                to_owner(me, peer).wait_send()

        @pl.when(me < owners)
        def _():
            for peer in others:
                from_owner(me, peer).wait_send()


def on_device(
    token_ids, embed_table, projected_table, feat_one, inner_taps, feat_two, decay, residue
):
    tokens = token_ids.shape[0]
    vocab, channels = embed_table.shape
    modes = decay.shape[1]
    count = lax.axis_size("ctx")
    peers = lax.axis_size("tp")
    steps = tokens // SEGMENTS
    keep = even(feat_two.shape[0] - 1)
    lead = even(keep + inner_taps.shape[0] - 1 + feat_one.shape[0] - 1)
    rows = (steps + keep) * SEGMENTS
    padded = -(-rows // LANES) * LANES
    earlier = lax.ppermute(token_ids, "ctx", [(source, source + 1) for source in range(count - 1)])
    feats = jnp.concatenate([feat_one, feat_two])
    rates = jnp.concatenate([jnp.transpose(decay), jnp.transpose(residue), inner_taps])
    proj = jnp.transpose(projected_table, (1, 0, 2))

    wide = min(512, channels)
    blocks = channels // wide
    extended = (steps + lead) * SEGMENTS
    size = max(4 * LANES, channels // count)
    owners = channels // size
    begun = blocks + 1 + owners
    whole = lambda shape: pl.BlockSpec(shape, lambda c: (0,) * len(shape))
    raw = pltpu.VMEM((4, wide // LANES, extended, LANES), jnp.float32)
    shared = lambda number: pltpu.VMEM((number, modes, size), jnp.float32)
    return pl.pallas_call(
        functools.partial(kernel, lead, keep, count, peers, channels * peers, modes),
        grid=(begun + owners,),
        in_specs=[
            whole((1, tokens)),
            whole((1, tokens)),
            pl.BlockSpec(memory_space=pl.ANY),
            pl.BlockSpec(memory_space=pl.ANY),
            whole(feats.shape),
            whole(rates.shape),
        ],
        out_specs=pl.BlockSpec((tokens, size), lambda c: (0, jnp.maximum(c - begun, 0))),
        out_shape=jax.ShapeDtypeStruct((tokens, channels), jnp.bfloat16),
        scratch_shapes=[
            pltpu.VMEM((channels // LANES, rows, LANES), jnp.bfloat16),
            pltpu.VMEM((SEGMENTS, padded), jnp.float32),
            raw,
            raw,
            pltpu.VMEM((padded, LANES), jnp.float32),
            pltpu.VMEM((LANES + tokens, LANES), jnp.float32),
            pltpu.VMEM((extended, vocab), jnp.bfloat16),
            pltpu.VMEM((blocks, 4, vocab, wide), jnp.bfloat16),
            pltpu.VMEM((padded, LANES), jnp.float32),
            pltpu.VMEM((peers, SEGMENTS, padded), jnp.float32),
            pltpu.VMEM((owners, size // LANES, tokens, LANES), jnp.float32),
            pltpu.VMEM((owners, size // LANES, modes, SEGMENTS, LANES), jnp.float32),
            shared(owners),
            shared(count),
            shared(count),
            shared(owners),
            pltpu.VMEM((tokens, LANES), jnp.float32),
            pltpu.VMEM((4, modes, LANES), jnp.float32),
            pltpu.VMEM((tokens, LANES), jnp.float32),
            pltpu.SemaphoreType.DMA((blocks, 2)),
            pltpu.SemaphoreType.DMA((peers,)),
            pltpu.SemaphoreType.DMA((peers,)),
        ]
        + [pltpu.SemaphoreType.DMA((count,))] * 4,
        compiler_params=pltpu.CompilerParams(
            dimension_semantics=("arbitrary",),
            collective_id=0,
            has_side_effects=True,
            vmem_limit_bytes=VMEM_LIMIT,
        ),
        name="hyena",
    )(
        earlier[None],
        token_ids[None],
        embed_table,
        proj,
        feats,
        rates,
    )


def solution(mesh):
    placed = (
        P("ctx"),
        P(None, "tp"),
        P(None, None, "tp"),
        P(None, None, "tp"),
        P(None, "tp"),
        P(None, None, "tp"),
        P("tp", None),
        P("tp", None),
    )
    return jax.shard_map(
        on_device, mesh=mesh, in_specs=placed, out_specs=P("ctx", "tp"), check_vma=False
    )
```
